128 devices in a mesh: seg: 16 (over y, z_lo, core), tile: 8 (over x, z_hi).
Axes of the slice: x: 4, y: 4, z: 4 (z_hi: 2, z_lo: 2; z = z_hi * 2 + z_lo), core: 2. Of those that a mesh axis runs over, the one named last changes fastest.
Arguments:
- path_field: float32 [128, 128, 64, 128], P('seg', 'tile'), may hold values from -1.2 to 1.2
- counts: int32 [16], replicated, may hold values from 0 to 16, as said below
- offsets: int32 [128], replicated, may hold values from 0 to 6
- weights: float32 [128], replicated, may hold values from 0 to 1
Outputs:
- new_path: float32 [128, 128, 64, 128], P('seg', 'tile')
The draws below stay inside these ranges and needn't reach their ends.
Inputs may be any that keep to these rules, and one draw needn't show every extreme that they name: counts sum to 128; for every segment s the running sum of counts before s differs from s * 8 by at most 4; the first segment supplies 8 + 8 // 2 new images, and a segment of 16 new images occurs in every draw.
All inputs are finite; a program needn't handle non-finite values.
Results may differ from the reference program's by a relative error of at most 0.00002.
Values sent between devices are 32-bit elements; how exact they have to be, the bound alone decides.
No kernel may reach another device: no remote copies, remote signals or barrier semaphores. Data moves between devices by JAX's collectives and lax.ppermute only.
A program may use at most 128 MiB of HBM per device.

```python
import jax
import jax.numpy as jnp

IMG = 8
GY = 64
GZ = 128
ITERS = 2
K = 128
GX = 128


def draw_counts(key, part):
    groups = K // IMG
    half_slots = IMG // 2
    key_shift, second = jax.random.split(jax.random.fold_in(key, 11))
    shifts = jax.random.randint(key_shift, (groups,), -half_slots, half_slots + 1)
    chosen = jax.random.randint(second, (), 1, groups - 2)
    places = jnp.arange(groups)
    shifts = jnp.where(places == 0, half_slots, shifts)
    shifts = jnp.where(places == chosen, -half_slots, shifts)
    shifts = jnp.where(places == chosen + 1, half_slots, shifts)
    shifts = jnp.where(places == groups - 1, 0, shifts)
    before = jnp.concatenate([jnp.zeros((1,), shifts.dtype), shifts[:-1]])
    return (IMG + shifts - before).astype(jnp.int32)


def touch_ends(drawn, stream_key, low, top_value):
    longest = drawn.shape.index(max(drawn.shape))
    spots = []
    for shift in (0, 1):
        where = [jax.random.randint(jax.random.fold_in(stream_key, axis), (), 0, length) for axis, length in enumerate(drawn.shape)]
        where[longest] = (where[longest] + shift) % drawn.shape[longest]
        spots.append(tuple(where))
    return drawn.at[spots[0]].set(low).at[spots[1]].set(top_value)


def block_scale(key, extent, pieces, least, largest):
    gain, own = 1.0, jax.random.fold_in(key, 6)
    for dim, shards_of in pieces:
        draws = jnp.exp(jax.random.uniform(jax.random.fold_in(own, dim), (shards_of,), jnp.float32, least / len(pieces), largest / len(pieces)))
        gain = gain * jnp.repeat(draws, extent[dim] // shards_of).reshape([-1 if axis == dim else 1 for axis in range(len(extent))])
    return gain


def setup_inputs(seed: int = 0) -> dict:
    keys = jax.random.split(jax.random.key(seed), 5)
    return {
        "path_field": jnp.clip(jax.random.uniform(keys[0], (K, GX, GY, GZ), jnp.float32, -1.2, 1.2) * block_scale(keys[0], (K, GX, GY, GZ), ((0, 16), (1, 8)), -0.4, 0.0), -1.2, 1.2),
        "counts": draw_counts(jax.random.fold_in(keys[4], 71), 0),
        "offsets": touch_ends(jax.random.randint(keys[2], (K,), 0, IMG - 1), jax.random.fold_in(keys[2], 1), 0, (IMG - 1) - 1).astype(jnp.int32),
        "weights": jnp.clip(jax.random.uniform(keys[3], (K,), jnp.float32, 0.0, 1.0), 0.0, 1.0),
    }


KAPPA_COEF = 1.0
TIME_STEP = 0.1
DESCENT_RATE = 0.01


def laplacian(field_in):
    padded = jnp.pad(field_in, ((0, 0), (1, 1), (0, 0), (0, 0)))
    summed = padded[:, 2:] + padded[:, :-2] - 6.0 * field_in
    for axis_num in (2, 3):
        summed = summed + jnp.roll(field_in, 1, axis_num) + jnp.roll(field_in, -1, axis_num)
    return summed


def drift_term(field_in):
    return KAPPA_COEF * laplacian(field_in) + field_in - field_in * field_in * field_in


def descent(current):
    count_all = current.shape[0]
    image_ids = jnp.arange(count_all, dtype=jnp.int32).reshape(-1, 1, 1, 1)
    ahead_images = jnp.concatenate([current[1:], jnp.zeros_like(current[:1])], 0)
    residual = (ahead_images - current) / TIME_STEP - drift_term(current)
    residual = jnp.where(image_ids == count_all - 1, jnp.zeros_like(residual), residual)
    behind = jnp.concatenate([jnp.zeros_like(residual[:1]), residual[:-1]], 0)
    gradient = behind - residual - TIME_STEP * (KAPPA_COEF * laplacian(residual) + (1.0 - 3.0 * current * current) * residual)
    interior = (image_ids > 0) & (image_ids < count_all - 1)
    return current - DESCENT_RATE * jnp.where(interior, gradient, jnp.zeros_like(gradient))


def reference(path_field, counts, offsets, weights):
    current = path_field
    for iteration in range(ITERS):
        current = descent(current)
    count_all = current.shape[0]
    run_ends = jnp.cumsum(counts).astype(jnp.int32)
    targets = jnp.arange(count_all, dtype=jnp.int32)
    source_seg = jnp.sum((run_ends[None, :] <= targets[:, None]).astype(jnp.int32), axis=1).astype(jnp.int32)
    source = (source_seg * IMG + offsets).astype(jnp.int32)
    lower_image = current[source]
    upper_image = current[source + 1]
    share_low = weights.reshape(-1, 1, 1, 1)
    return share_low * lower_image + (1.0 - share_low) * upper_image
```

```python
import functools

import jax
import jax.numpy as jnp
from jax import lax
from jax.experimental import pallas as pl
from jax.experimental.pallas import tpu as pltpu
from jax.sharding import PartitionSpec as P

KAPPA_COEF = 1.0
TIME_STEP = 0.1
DESCENT_RATE = 0.01


AXES = ("seg", "tile")
ANY = pl.BlockSpec(memory_space=pl.ANY)
VMEM = pl.BlockSpec(memory_space=pltpu.VMEM)
SMEM = pl.BlockSpec(memory_space=pltpu.SMEM)


def routes(segs, tiles, ds_of, dt):
    pairs = []
    for s in range(segs):
        for t in range(tiles):
            to_s, to_t = s + ds_of(s), t + dt
            if 0 <= to_s < segs and 0 <= to_t < tiles:
                pairs.append((s * tiles + t, to_s * tiles + to_t))
    return pairs


def outer(s):
    return 1 if s % 2 else -1


def inner(s):
    return -1 if s % 2 else 1


def shifted_sum(ref, j, x, c):
    total = ref[j, x + 1] + ref[j, x - 1] - 6.0 * c
    for axis in (0, 1):
        total = total + pltpu.roll(c, 1, axis) + pltpu.roll(c, c.shape[axis] - 1, axis)
    return total


def each_plane(images, planes, body):
    def over_images(j, carry):
        def over_planes(x, inner_carry):
            body(j, x)
            return inner_carry

        return lax.fori_loop(planes[0], planes[1], over_planes, carry, unroll=2)

    lax.fori_loop(images[0], images[1], over_images, 0)


def residual_stage(p, r, images, planes):
    def body(j, x):
        c = p[j, x]
        drift = KAPPA_COEF * shifted_sum(p, j, x, c) + c - c * c * c
        r[j, x] = (p[j + 1, x] - c) * (1.0 / TIME_STEP) - drift

    each_plane(images, planes, body)


def update_stage(p, r, images, planes, first_id, last_id):
    def body(j, x):
        c = p[j, x]
        rc = r[j, x]
        pull = KAPPA_COEF * shifted_sum(r, j, x, rc) + (1.0 - 3.0 * c * c) * rc
        gradient = r[j - 1, x] - rc - TIME_STEP * pull
        image_id = first_id + j
        rate = jnp.where((image_id > 0) & (image_id < last_id), DESCENT_RATE, 0.0)
        p[j, x] = c - rate * gradient

    each_plane(images, planes, body)


def clear(ref, images, planes):
    def body(j, x):
        ref[j, x] = jnp.zeros(ref.shape[2:], ref.dtype)

    each_plane(images, planes, body)


def descend(p, r, images, s, segs, outside):
    n = p.shape[1]
    first_id, last_id = s * images - 2, segs * images - 1
    for step in range(2):
        lo, hi = 2 * step + 1, n - 2 * step - 1
        residual_stage(p, r, (step, images + 3 - step), (lo, hi))

        @pl.when(s == 0)
        def _():
            clear(r, (step, 2), (lo, hi))

        @pl.when(s == segs - 1)
        def _():
            clear(r, (images + 1, images + 3 - step), (lo, hi))

        for cond, planes in outside:

            @pl.when(cond)
            def _(planes=planes):
                clear(r, (step, images + 3 - step), planes)

        update_stage(
            p, r, (step + 1, images + 3 - step), (lo + 1, hi - 1), first_id, last_id
        )
        if step == 0:
            for cond, planes in outside:

                @pl.when(cond)
                def _(planes=planes):
                    clear(p, (1, images + 3), planes)


def mix(weights, offsets, k, p, base, x):
    w = weights[k]
    q = offsets[k] + base
    return w * p[q, x] + (1.0 - w) * p[q + 1, x]


def run_copies(copies):
    for c in copies:
        c.start()
    for c in copies:
        c.wait()


def outer_base(s, images):
    core = lax.rem(s, 2)
    half = images // 2
    k = jnp.where(core == 0, s * images - half, (s + 1) * images)
    return jnp.clip(k, 0, None)


def inner_base(s, images):
    core = lax.rem(s, 2)
    half = images // 2
    return jnp.where(core == 0, (s + 1) * images, s * images - half)


def inside_kernel(
    segs, place, offsets, weights, path, from_outer, from_inner, p2, slots, p, r, sems
):
    images, n = path.shape[0], path.shape[1]
    s = place[0]
    core = lax.rem(s, 2)
    run_copies(
        [
            pltpu.make_async_copy(path, p.at[pl.ds(2, images)], sems.at[0]),
            pltpu.make_async_copy(
                from_outer, p.at[pl.ds(jnp.where(core == 0, 0, images + 2), 2)], sems.at[1]
            ),
            pltpu.make_async_copy(
                from_inner, p.at[pl.ds(jnp.where(core == 0, images + 2, 0), 2)], sems.at[2]
            ),
        ]
    )
    descend(p, r, images, s, segs, ())
    half = images // 2
    total = segs * images
    k0 = outer_base(s, images)

    def to_slots(i, x):
        k = jnp.minimum(k0 + i, total - 1)
        slots[i, x] = mix(weights, offsets, k, p, 2, x + 4)

    each_plane((0, half), (0, n - 8), to_slots)

    def to_p2(j, x):
        p2[j, x] = p[j + 2, x + 4]

    each_plane((0, images), (0, n - 8), to_p2)


def edge_kernel(
    segs,
    tiles,
    place,
    offsets,
    weights,
    path,
    from_outer,
    from_inner,
    below,
    above,
    corner_below,
    corner_above,
    corner_inner,
    p2,
    slots,
    p_low,
    p_high,
    r,
    sems,
):
    images, n = path.shape[0], path.shape[1]
    s, t = place[0], place[1]
    core = lax.rem(s, 2)
    outer_row = jnp.where(core == 0, 0, images + 2)
    inner_row = jnp.where(core == 0, images + 2, 0)
    outer_near = jnp.where(core == 0, 1, images + 2)
    outer_far = jnp.where(core == 0, 0, images + 3)
    inner_near = jnp.where(core == 0, images + 2, 1)
    inner_far = jnp.where(core == 0, images + 3, 0)
    plan = []
    for p, own, at in ((p_low, pl.ds(0, 8), pl.ds(4, 8)), (p_high, pl.ds(n - 8, 8), pl.ds(0, 8))):
        plan += [
            (path.at[:, own], p.at[pl.ds(2, images), at]),
            (from_outer.at[:, own], p.at[pl.ds(outer_row, 2), at]),
            (from_inner.at[:, own], p.at[pl.ds(inner_row, 2), at]),
        ]
    plan += [
        (below, p_low.at[pl.ds(2, images), pl.ds(0, 4)]),
        (above, p_high.at[pl.ds(2, images), pl.ds(8, 4)]),
        (corner_below.at[pl.ds(0, 3)], p_low.at[outer_near, pl.ds(1, 3)]),
        (corner_below.at[pl.ds(3, 2)], p_low.at[outer_far, pl.ds(2, 2)]),
        (corner_above.at[pl.ds(0, 3)], p_high.at[outer_near, pl.ds(8, 3)]),
        (corner_above.at[pl.ds(3, 2)], p_high.at[outer_far, pl.ds(8, 2)]),
        (corner_inner.at[pl.ds(0, 3)], p_low.at[inner_near, pl.ds(1, 3)]),
        (corner_inner.at[pl.ds(3, 2)], p_low.at[inner_far, pl.ds(2, 2)]),
        (corner_inner.at[pl.ds(5, 3)], p_high.at[inner_near, pl.ds(8, 3)]),
        (corner_inner.at[pl.ds(8, 2)], p_high.at[inner_far, pl.ds(8, 2)]),
    ]
    run_copies([pltpu.make_async_copy(a, b, sems.at[i]) for i, (a, b) in enumerate(plan)])
    half = images // 2
    total = segs * images
    k0 = outer_base(s, images)
    for p, start, outside in (
        (p_low, 0, ((t == 0, (1, 4)),)),
        (p_high, 4, ((t == tiles - 1, (8, 11)),)),
    ):
        descend(p, r, images, s, segs, outside)

        def to_slots(i, x):
            k = jnp.minimum(k0 + i, total - 1)
            slots[i, x + start] = mix(weights, offsets, k, p, 2, x + 4)

        each_plane((0, half), (0, 4), to_slots)

        def to_p2(j, x):
            p2[j, x + start] = p[j + 2, x + 4]

        each_plane((0, images), (0, 4), to_p2)


def plane_parts(n):
    return ((0, 4, 0, 0), (4, n - 4, 1, 0), (n - 4, n, 0, 4))


def inner_slots_kernel(segs, place, offsets, weights, p2_edge, p2_inside, slots):
    images, n = p2_edge.shape[0], slots.shape[1]
    half = images // 2
    k0 = inner_base(place[0], images)
    for lo, hi, which, start in plane_parts(n):
        p = (p2_edge, p2_inside)[which]

        def body(i, x):
            slots[i, x + lo] = mix(weights, offsets, k0 + i, p, 0, x + start)

        each_plane((0, half), (0, hi - lo), body)


def own_kernel(place, offsets, weights, p2_edge, p2_inside, out):
    images, n = out.shape[0], out.shape[1]
    k0 = place[0] * images
    for lo, hi, which, start in plane_parts(n):
        p = (p2_edge, p2_inside)[which]

        def body(i, x):
            out[i, x + lo] = mix(weights, offsets, k0 + i, p, 0, x + start)

        each_plane((0, images), (0, hi - lo), body)


def source_step(counts, k, s, segs):
    end = jnp.int32(0)
    source = jnp.int32(0)
    for i in range(segs):
        end = end + counts[i]
        source = source + jnp.where(end <= k, 1, 0)
    return source - s


def place_kernel(segs, place, counts, edge, inside, inner_part, own, out, sems):
    del own
    images, n = out.shape[0], out.shape[1]
    half = images // 2
    s = place[0]
    core = lax.rem(s, 2)

    def copies(i, slot, from_outer):
        for lo, hi, which, start in plane_parts(n):
            if from_outer:
                src = (edge, inside)[which].at[slot, pl.ds(start, hi - lo)]
            else:
                src = inner_part.at[slot, pl.ds(lo, hi - lo)]
            yield pltpu.make_async_copy(src, out.at[i, pl.ds(lo, hi - lo)], sems.at[i])

    for start in (True, False):
        for i in range(images):
            step = source_step(counts, s * images + i, s, segs)
            slot = i % half
            foreign = (step < 0) if i < half else (step > 0)
            outer_core = 0 if i < half else 1

            for from_outer in (True, False):

                @pl.when(foreign & ((core == outer_core) == from_outer))
                def _(i=i, slot=slot, from_outer=from_outer):
                    for c in copies(i, slot, from_outer):
                        if start:
                            c.start()
                        else:
                            c.wait()


def field(*shape):
    return jax.ShapeDtypeStruct(shape, jnp.float32)


def cost(planes, arrays):
    return pl.CostEstimate(
        flops=planes * 8192 * 60, bytes_accessed=arrays * 2**20, transcendentals=0
    )


def local(path_field, counts, offsets, weights):
    images, n, gy, gz = path_field.shape
    segs, tiles = lax.axis_size("seg"), lax.axis_size("tile")
    s, t = lax.axis_index("seg"), lax.axis_index("tile")
    core = lax.rem(s, 2)
    half = images // 2
    place = jnp.stack([s, t]).astype(jnp.int32)

    def send(block, ds_of, dt):
        return lax.ppermute(block, AXES, routes(segs, tiles, ds_of, dt))

    def stay(_):
        return 0

    def images_from(first_if_zero, first_if_one, array, count):
        return lax.dynamic_slice_in_dim(
            array, jnp.where(core == 0, first_if_zero, first_if_one), count, 0
        )

    def corner(array, near_if_zero, low):
        pair = images_from(0 if near_if_zero == 0 else images - 2, images - 2 if near_if_zero == 0 else 0, array, 2)
        is_first = (core == 0) if near_if_zero == 0 else (core == 1)
        near = jnp.where(is_first, pair[0], pair[1])
        far = jnp.where(is_first, pair[1], pair[0])
        width = array.shape[1]
        if low:
            return jnp.concatenate([near[:3], far[:2]], 0)
        return jnp.concatenate([near[width - 3 :], far[width - 2 :]], 0)

    from_outer = send(images_from(0, images - 2, path_field, 2), outer, 0)
    from_inner = send(images_from(images - 2, 0, path_field, 2), inner, 0)
    below = send(path_field[:, n - 4 :], stay, 1)
    above = send(path_field[:, :4], stay, -1)
    corner_below = send(corner(path_field, 0, False), outer, 1)
    corner_above = send(corner(path_field, 0, True), outer, -1)

    inside_params = dict(
        out_shape=(field(images, n - 8, gy, gz), field(half, n - 8, gy, gz)),
        in_specs=[SMEM, SMEM, SMEM, ANY, ANY, ANY],
        out_specs=(VMEM, VMEM),
        scratch_shapes=[
            pltpu.VMEM((images + 4, n, gy, gz), jnp.float32),
            pltpu.VMEM((images + 3, n, gy, gz), jnp.float32),
            pltpu.SemaphoreType.DMA((3,)),
        ],
        cost_estimate=cost(44 * 10, 8),
    )
    p2_inside, slots_inside = pl.pallas_call(
        functools.partial(inside_kernel, segs), name="inside", **inside_params
    )(place, offsets, weights, path_field, from_outer, from_inner)
    got_inside = send(slots_inside, outer, 0)

    corner_inner = send(
        jnp.concatenate(
            [corner(below, images - 1, False), corner(above, images - 1, True)], 0
        ),
        inner,
        0,
    )
    p2_edge, slots_edge = pl.pallas_call(
        functools.partial(edge_kernel, segs, tiles),
        name="edge",
        out_shape=(field(images, 8, gy, gz), field(half, 8, gy, gz)),
        in_specs=[SMEM, SMEM, SMEM] + [ANY] * 8,
        out_specs=(VMEM, VMEM),
        scratch_shapes=[
            pltpu.VMEM((images + 4, 12, gy, gz), jnp.float32),
            pltpu.VMEM((images + 4, 12, gy, gz), jnp.float32),
            pltpu.VMEM((images + 3, 12, gy, gz), jnp.float32),
            pltpu.SemaphoreType.DMA((16,)),
        ],
        cost_estimate=cost(56 * 10, 10),
    )(
        place,
        offsets,
        weights,
        path_field,
        from_outer,
        from_inner,
        below,
        above,
        corner_below,
        corner_above,
        corner_inner,
    )
    got_edge = send(slots_edge, outer, 0)
    slots_inner = pl.pallas_call(
        functools.partial(inner_slots_kernel, segs),
        name="inner_slots",
        out_shape=field(half, n, gy, gz),
        in_specs=[SMEM, SMEM, SMEM, VMEM, VMEM],
        out_specs=VMEM,
        cost_estimate=cost(16, 6),
    )(place, offsets, weights, p2_edge, p2_inside)
    got_inner = send(slots_inner, inner, 0)
    own = pl.pallas_call(
        own_kernel,
        name="own",
        out_shape=field(images, n, gy, gz),
        in_specs=[SMEM, SMEM, SMEM, VMEM, VMEM],
        out_specs=VMEM,
        cost_estimate=cost(32, 8),
    )(place, offsets, weights, p2_edge, p2_inside)
    return pl.pallas_call(
        functools.partial(place_kernel, segs),
        name="place",
        out_shape=field(images, n, gy, gz),
        in_specs=[SMEM, SMEM, VMEM, VMEM, VMEM, ANY],
        out_specs=ANY,
        scratch_shapes=[pltpu.SemaphoreType.DMA((images,))],
        input_output_aliases={5: 0},
        cost_estimate=cost(2, 4),
    )(place, counts, got_edge, got_inside, got_inner, own)


def solution(mesh):
    return jax.shard_map(
        local,
        mesh=mesh,
        in_specs=(P("seg", "tile", None, None), P(), P(), P()),
        out_specs=P("seg", "tile", None, None),
        check_vma=False,
    )
```

```python
import functools

import jax
import jax.numpy as jnp
from jax import lax
from jax.experimental import pallas as pl
from jax.experimental.pallas import tpu as pltpu
from jax.sharding import PartitionSpec as P


KAPPA_COEF = 1.0
TIME_STEP = 0.1
DESCENT_RATE = 0.01


AXES = ("seg", "tile")
ANY = pl.BlockSpec(memory_space=pl.ANY)
VMEM = pl.BlockSpec(memory_space=pltpu.VMEM)
SMEM = pl.BlockSpec(memory_space=pltpu.SMEM)


def routes(segs, tiles, ds_of, dt):
    pairs = []
    for s in range(segs):
        for t in range(tiles):
            to_s, to_t = s + ds_of(s), t + dt
            if 0 <= to_s < segs and 0 <= to_t < tiles:
                pairs.append((s * tiles + t, to_s * tiles + to_t))
    return pairs


def outer(s):
    return 1 if s % 2 else -1


def inner(s):
    return -1 if s % 2 else 1


def neighbour_sum(ref, j, x, c):
    total = ref[j, x + 1] + ref[j, x - 1]
    for axis in (0, 1):
        total = total + (pltpu.roll(c, 1, axis) + pltpu.roll(c, c.shape[axis] - 1, axis))
    return total


def each_plane(images, planes, body):
    def over_images(j, carry):
        def over_planes(x, inner_carry):
            body(j, x)
            return inner_carry

        return lax.fori_loop(planes[0], planes[1], over_planes, carry, unroll=planes[1] - planes[0])

    lax.fori_loop(images[0], images[1], over_images, 0)


def residual_stage(p, r, images, planes):
    def body(j, x):
        c = p[j, x]
        linear = 6.0 * KAPPA_COEF - 1.0 - 1.0 / TIME_STEP
        total = neighbour_sum(p, j, x, c)
        if KAPPA_COEF != 1.0:
            total = KAPPA_COEF * total
        r[j, x] = p[j + 1, x] * (1.0 / TIME_STEP) - total + c * (c * c + linear)

    each_plane(images, planes, body)


def update_stage(p, r, images, planes, first_id, last_id):
    def body(j, x):
        c = p[j, x]
        rc = r[j, x]
        linear = 1.0 + TIME_STEP * (1.0 - 6.0 * KAPPA_COEF)
        pull = rc * (linear - (3.0 * TIME_STEP) * (c * c)) - r[j - 1, x]
        down = (TIME_STEP * KAPPA_COEF) * neighbour_sum(r, j, x, rc) + pull
        image_id = first_id + j
        rate = jnp.where((image_id > 0) & (image_id < last_id), DESCENT_RATE, 0.0)
        p[j, x] = c + rate * down

    each_plane(images, planes, body)


def clear(ref, images, planes):
    def body(j, x):
        ref[j, x] = jnp.zeros(ref.shape[2:], ref.dtype)

    each_plane(images, planes, body)


def descend(p, r, images, s, segs, outside):
    n = p.shape[1]
    first_id, last_id = s * images - 2, segs * images - 1
    for step in range(2):
        lo, hi = 2 * step + 1, n - 2 * step - 1
        residual_stage(p, r, (step, images + 3 - step), (lo, hi))

        @pl.when(s == 0)
        def _():
            clear(r, (step, 2), (lo, hi))

        @pl.when(s == segs - 1)
        def _():
            clear(r, (images + 1, images + 3 - step), (lo, hi))

        for cond, planes in outside:

            @pl.when(cond)
            def _(planes=planes):
                clear(r, (step, images + 3 - step), planes)

        update_stage(
            p, r, (step + 1, images + 3 - step), (lo + 1, hi - 1), first_id, last_id
        )
        if step == 0:
            for cond, planes in outside:

                @pl.when(cond)
                def _(planes=planes):
                    clear(p, (1, images + 3), planes)


def mix(weights, offsets, k, p, base, x):
    w = weights[k]
    q = offsets[k] + base
    return w * p[q, x] + (1.0 - w) * p[q + 1, x]


def run_copies(copies):
    for c in copies:
        c.start()
    for c in copies:
        c.wait()


def outer_base(s, images):
    core = lax.rem(s, 2)
    half = images // 2
    k = jnp.where(core == 0, s * images - half, (s + 1) * images)
    return jnp.clip(k, 0, None)


def inner_base(s, images):
    core = lax.rem(s, 2)
    half = images // 2
    return jnp.where(core == 0, (s + 1) * images, s * images - half)


def inside_kernel(
    segs, place, offsets, weights, path, from_outer, from_inner, p2, slots, p, r, sems
):
    images, n = path.shape[0], path.shape[1]
    s = place[0]
    core = lax.rem(s, 2)
    run_copies(
        [
            pltpu.make_async_copy(path, p.at[pl.ds(2, images)], sems.at[0]),
            pltpu.make_async_copy(
                from_outer, p.at[pl.ds(jnp.where(core == 0, 0, images + 2), 2)], sems.at[1]
            ),
            pltpu.make_async_copy(
                from_inner, p.at[pl.ds(jnp.where(core == 0, images + 2, 0), 2)], sems.at[2]
            ),
        ]
    )
    descend(p, r, images, s, segs, ())
    half = images // 2
    total = segs * images
    k0 = outer_base(s, images)

    def to_slots(i, x):
        k = jnp.minimum(k0 + i, total - 1)
        slots[i, x] = mix(weights, offsets, k, p, 2, x + 4)

    each_plane((0, half), (0, n - 8), to_slots)

    def to_p2(j, x):
        p2[j, x] = p[j + 2, x + 4]

    each_plane((0, images), (0, n - 8), to_p2)


def edge_kernel(
    segs,
    tiles,
    low,
    place,
    offsets,
    weights,
    path,
    from_outer,
    from_inner,
    beyond,
    corner_outer,
    corner_inner,
    p2,
    slots,
    p,
    r,
    sems,
):
    images, n = path.shape[0], path.shape[1]
    s, t = place[0], place[1]
    core = lax.rem(s, 2)
    outer_near = jnp.where(core == 0, 1, images + 2)
    outer_far = jnp.where(core == 0, 0, images + 3)
    inner_near = jnp.where(core == 0, images + 2, 1)
    inner_far = jnp.where(core == 0, images + 3, 0)
    outer_row = jnp.where(core == 0, 0, images + 2)
    inner_row = jnp.where(core == 0, images + 2, 0)
    own, at = (pl.ds(0, 8), pl.ds(4, 8)) if low else (pl.ds(n - 8, 8), pl.ds(0, 8))
    three, two = (pl.ds(1, 3), pl.ds(2, 2)) if low else (pl.ds(8, 3), pl.ds(8, 2))
    plan = [
        (path.at[:, own], p.at[pl.ds(2, images), at]),
        (from_outer.at[:, own], p.at[pl.ds(outer_row, 2), at]),
        (from_inner.at[:, own], p.at[pl.ds(inner_row, 2), at]),
        (beyond, p.at[pl.ds(2, images), pl.ds(0 if low else 8, 4)]),
        (corner_outer.at[pl.ds(0, 3)], p.at[outer_near, three]),
        (corner_outer.at[pl.ds(3, 2)], p.at[outer_far, two]),
        (corner_inner.at[pl.ds(0, 3)], p.at[inner_near, three]),
        (corner_inner.at[pl.ds(3, 2)], p.at[inner_far, two]),
    ]
    run_copies([pltpu.make_async_copy(a, b, sems.at[i]) for i, (a, b) in enumerate(plan)])
    half = images // 2
    total = segs * images
    k0 = outer_base(s, images)
    outside = (t == 0, (1, 4)) if low else (t == tiles - 1, (8, 11))
    descend(p, r, images, s, segs, (outside,))

    def to_slots(i, x):
        k = jnp.minimum(k0 + i, total - 1)
        slots[i, x] = mix(weights, offsets, k, p, 2, x + 4)

    each_plane((0, half), (0, 4), to_slots)

    def to_p2(j, x):
        p2[j, x] = p[j + 2, x + 4]

    each_plane((0, images), (0, 4), to_p2)


def corner_kernel(low, first_if_zero, place, src, out, sems):
    images, width = src.shape[0], src.shape[1]
    at_first = (lax.rem(place[0], 2) == 0) == first_if_zero
    near = jnp.where(at_first, 0, images - 1)
    far = jnp.where(at_first, 1, images - 2)
    three, two = (pl.ds(0, 3), pl.ds(0, 2)) if low else (pl.ds(width - 3, 3), pl.ds(width - 2, 2))
    run_copies(
        [
            pltpu.make_async_copy(src.at[near, three], out.at[pl.ds(0, 3)], sems.at[0]),
            pltpu.make_async_copy(src.at[far, two], out.at[pl.ds(3, 2)], sems.at[1]),
        ]
    )


def pair_kernel(first_if_zero, place, path, out, sems):
    images = path.shape[0]
    at_first = (lax.rem(place[0], 2) == 0) == first_if_zero
    first = jnp.where(at_first, 0, images - 2)
    run_copies([pltpu.make_async_copy(path.at[pl.ds(first, 2)], out, sems.at[0])])


def plane_parts(n):
    return ((0, 4, 0), (4, n - 4, 1), (n - 4, n, 2))


def inner_slots_kernel(place, offsets, weights, low, inside, high, slots):
    images, n = inside.shape[0], slots.shape[1]
    half = images // 2
    k0 = inner_base(place[0], images)
    for lo, hi, which in plane_parts(n):
        p = (low, inside, high)[which]

        def body(i, x):
            slots[i, x + lo] = mix(weights, offsets, k0 + i, p, 0, x)

        each_plane((0, half), (0, hi - lo), body)


def own_kernel(place, offsets, weights, low, inside, high, out):
    images, n = out.shape[0], out.shape[1]
    k0 = place[0] * images
    for lo, hi, which in plane_parts(n):
        p = (low, inside, high)[which]

        def body(i, x):
            out[i, x + lo] = mix(weights, offsets, k0 + i, p, 0, x)

        each_plane((0, images), (0, hi - lo), body)


def source_step(counts, k, s, segs):
    end = jnp.int32(0)
    source = jnp.int32(0)
    for i in range(segs):
        end = end + counts[i]
        source = source + jnp.where(end <= k, 1, 0)
    return source - s


def place_kernel(segs, place, counts, low, inside, high, inner_part, own, out, sems):
    del own
    images, n = out.shape[0], out.shape[1]
    half = images // 2
    s = place[0]
    core = lax.rem(s, 2)

    def copies(i, slot, from_outer):
        for lo, hi, which in plane_parts(n):
            if from_outer:
                src = (low, inside, high)[which].at[slot]
            else:
                src = inner_part.at[slot, pl.ds(lo, hi - lo)]
            yield pltpu.make_async_copy(src, out.at[i, pl.ds(lo, hi - lo)], sems.at[i, which])

    for start in (True, False):
        for i in range(images):
            step = source_step(counts, s * images + i, s, segs)
            slot = i % half
            foreign = (step < 0) if i < half else (step > 0)
            outer_core = 0 if i < half else 1

            for from_outer in (True, False):

                @pl.when(foreign & ((core == outer_core) == from_outer))
                def _(i=i, slot=slot, from_outer=from_outer):
                    for c in copies(i, slot, from_outer):
                        if start:
                            c.start()
                        else:
                            c.wait()


def field(*shape):
    return jax.ShapeDtypeStruct(shape, jnp.float32)


def cost(planes, arrays):
    return pl.CostEstimate(
        flops=planes * 8192 * 60, bytes_accessed=arrays * 2**20, transcendentals=0
    )


def params(mib):
    return pltpu.CompilerParams(vmem_limit_bytes=mib * 2**20)


def step(path_field, counts, offsets, weights):
    images, n, gy, gz = path_field.shape
    segs, tiles = lax.axis_size("seg"), lax.axis_size("tile")
    s, t = lax.axis_index("seg"), lax.axis_index("tile")
    half = images // 2
    place = jnp.stack([s, t]).astype(jnp.int32)

    def send(block, ds_of, dt):
        return lax.ppermute(block, AXES, routes(segs, tiles, ds_of, dt))

    def stay(_):
        return 0

    def call(kernel, *args, **settings):
        return pl.pallas_call(kernel, **settings)(*args)

    def corner(array, low, first_if_zero):
        return call(
            functools.partial(corner_kernel, low, first_if_zero),
            place,
            array,
            out_shape=field(5, gy, gz),
            in_specs=[SMEM, ANY],
            out_specs=VMEM,
            scratch_shapes=[pltpu.SemaphoreType.DMA((2,))],
            compiler_params=params(1),
            cost_estimate=cost(0, 1),
        )

    def pair(first_if_zero):
        return call(
            functools.partial(pair_kernel, first_if_zero),
            place,
            path_field,
            out_shape=field(2, n, gy, gz),
            in_specs=[SMEM, ANY],
            out_specs=VMEM,
            scratch_shapes=[pltpu.SemaphoreType.DMA((1,))],
            compiler_params=params(2),
            cost_estimate=cost(0, 2),
        )

    from_outer = send(pair(True), outer, 0)
    from_inner = send(pair(False), inner, 0)
    below = send(path_field[:, n - 4 :], stay, 1)
    above = send(path_field[:, :4], stay, -1)
    corner_below = send(corner(path_field, False, True), outer, 1)
    corner_above = send(corner(path_field, True, True), outer, -1)

    p2_inside, slots_inside = call(
        functools.partial(inside_kernel, segs),
        place,
        offsets,
        weights,
        path_field,
        from_outer,
        from_inner,
        out_shape=(field(images, n - 8, gy, gz), field(half, n - 8, gy, gz)),
        in_specs=[SMEM, SMEM, SMEM, ANY, ANY, ANY],
        out_specs=(VMEM, VMEM),
        scratch_shapes=[
            pltpu.VMEM((images + 4, n, gy, gz), jnp.float32),
            pltpu.VMEM((images + 3, n, gy, gz), jnp.float32),
            pltpu.SemaphoreType.DMA((3,)),
        ],
        compiler_params=params(18),
        cost_estimate=cost(44 * 10, 8),
    )
    got_inside = send(slots_inside, outer, 0)

    def edge(low, beyond, corner_outer):
        corner_inner = send(corner(beyond, not low, False), inner, 0)
        return call(
            functools.partial(edge_kernel, segs, tiles, low),
            place,
            offsets,
            weights,
            path_field,
            from_outer,
            from_inner,
            beyond,
            corner_outer,
            corner_inner,
            out_shape=(field(images, 4, gy, gz), field(half, 4, gy, gz)),
            in_specs=[SMEM, SMEM, SMEM] + [ANY] * 6,
            out_specs=(VMEM, VMEM),
            scratch_shapes=[
                pltpu.VMEM((images + 4, 12, gy, gz), jnp.float32),
                pltpu.VMEM((images + 3, 12, gy, gz), jnp.float32),
                pltpu.SemaphoreType.DMA((8,)),
            ],
            compiler_params=params(14),
            cost_estimate=cost(28 * 10, 6),
        )

    p2_low, slots_low = edge(True, below, corner_below)
    got_low = send(slots_low, outer, 0)
    p2_high, slots_high = edge(False, above, corner_above)
    got_high = send(slots_high, outer, 0)

    slots_inner = call(
        inner_slots_kernel,
        place,
        offsets,
        weights,
        p2_low,
        p2_inside,
        p2_high,
        out_shape=field(half, n, gy, gz),
        in_specs=[SMEM, SMEM, SMEM, VMEM, VMEM, VMEM],
        out_specs=VMEM,
        compiler_params=params(8),
        cost_estimate=cost(16, 6),
    )
    got_inner = send(slots_inner, inner, 0)
    own = call(
        own_kernel,
        place,
        offsets,
        weights,
        p2_low,
        p2_inside,
        p2_high,
        out_shape=field(images, n, gy, gz),
        in_specs=[SMEM, SMEM, SMEM, VMEM, VMEM, VMEM],
        out_specs=VMEM,
        compiler_params=params(10),
        cost_estimate=cost(32, 8),
    )
    return call(
        functools.partial(place_kernel, segs),
        place,
        counts,
        got_low,
        got_inside,
        got_high,
        got_inner,
        own,
        out_shape=field(images, n, gy, gz),
        in_specs=[SMEM, SMEM, VMEM, VMEM, VMEM, VMEM, ANY],
        out_specs=ANY,
        scratch_shapes=[pltpu.SemaphoreType.DMA((images, 3))],
        input_output_aliases={6: 0},
        compiler_params=params(6),
        cost_estimate=cost(2, 4),
    )


def solution(mesh):
    return jax.shard_map(
        step,
        mesh=mesh,
        in_specs=(P("seg", "tile", None, None), P(), P(), P()),
        out_specs=P("seg", "tile", None, None),
        check_vma=False,
    )
```

```python
import functools

import jax
import jax.numpy as jnp
from jax import lax
from jax.experimental import pallas as pl
from jax.experimental.pallas import tpu as pltpu
from jax.sharding import PartitionSpec as P


KAPPA_COEF = 1.0
TIME_STEP = 0.1
DESCENT_RATE = 0.01


AXES = ("seg", "tile")
ANY = pl.BlockSpec(memory_space=pl.ANY)
VMEM = pl.BlockSpec(memory_space=pltpu.VMEM)
SMEM = pl.BlockSpec(memory_space=pltpu.SMEM)


def routes(segs, tiles, ds_of, dt):
    pairs = []
    for s in range(segs):
        for t in range(tiles):
            to_s, to_t = s + ds_of(s), t + dt
            if 0 <= to_s < segs and 0 <= to_t < tiles:
                pairs.append((s * tiles + t, to_s * tiles + to_t))
    return pairs


def outer(s):
    return 1 if s % 2 else -1


def inner(s):
    return -1 if s % 2 else 1


def neighbour_sum(ref, j, x, c):
    total = ref[j, x + 1] + ref[j, x - 1]
    for axis in (0, 1):
        total = total + (pltpu.roll(c, 1, axis) + pltpu.roll(c, c.shape[axis] - 1, axis))
    return total


def each_plane(images, planes, body):
    def over_images(j, carry):
        def over_planes(x, inner_carry):
            body(j, x)
            return inner_carry

        return lax.fori_loop(planes[0], planes[1], over_planes, carry, unroll=planes[1] - planes[0])

    lax.fori_loop(images[0], images[1], over_images, 0)


def residual_stage(p, r, images, planes):
    def body(j, x):
        c = p[j, x]
        linear = 6.0 * KAPPA_COEF - 1.0 - 1.0 / TIME_STEP
        total = neighbour_sum(p, j, x, c)
        if KAPPA_COEF != 1.0:
            total = KAPPA_COEF * total
        r[j, x] = p[j + 1, x] * (1.0 / TIME_STEP) - total + c * (c * c + linear)

    each_plane(images, planes, body)


def update_stage(p, r, images, planes, first_id, last_id):
    def body(j, x):
        c = p[j, x]
        rc = r[j, x]
        linear = 1.0 + TIME_STEP * (1.0 - 6.0 * KAPPA_COEF)
        pull = rc * (linear - (3.0 * TIME_STEP) * (c * c)) - r[j - 1, x]
        down = (TIME_STEP * KAPPA_COEF) * neighbour_sum(r, j, x, rc) + pull
        image_id = first_id + j
        rate = jnp.where((image_id > 0) & (image_id < last_id), DESCENT_RATE, 0.0)
        p[j, x] = c + rate * down

    each_plane(images, planes, body)


def clear(ref, images, planes):
    def body(j, x):
        ref[j, x] = jnp.zeros(ref.shape[2:], ref.dtype)

    each_plane(images, planes, body)


def descend(p, r, images, s, segs, ranges, rows, outside):
    first_id, last_id = s * images - 2, segs * images - 1
    for step in range(2):
        at, moved = ranges[step]
        residual_rows, update_rows = rows[step]
        residual_stage(p, r, residual_rows, at)

        @pl.when(s == 0)
        def _():
            clear(r, (step, 2), at)

        @pl.when(s == segs - 1)
        def _():
            clear(r, (images + 1, images + 3 - step), at)

        for cond, planes in outside:

            @pl.when(cond)
            def _(planes=planes):
                clear(r, residual_rows, planes)

        update_stage(p, r, update_rows, moved, first_id, last_id)
        if step == 0:
            for cond, planes in outside:

                @pl.when(cond)
                def _(planes=planes):
                    clear(p, update_rows, planes)


def all_rows(images):
    return (
        ((0, images + 3), (1, images + 3)),
        ((1, images + 2), (2, images + 2)),
    )


def inner_rows(images, core):
    a = jnp.where(core == 0, 2, 0)
    return (
        ((a, a + images + 1), (a + 1, a + images + 1)),
        ((a + 1, a + images), (a + 2, a + images)),
    )


def outer_rows(images, core):
    starts = [jnp.where(core == 0, a, images + b) for a, b in ((0, 1), (1, 1), (1, 0), (2, 0))]
    first, second, third, fourth = [(a, a + 2) for a in starts]
    return ((first, second), (third, fourth))


def inside_ranges(n):
    return (((1, n - 1), (2, n - 2)), ((3, n - 3), (4, n - 4)))


def mix(weights, offsets, k, p, base, x):
    w = weights[k]
    q = offsets[k] + base
    return w * p[q, x] + (1.0 - w) * p[q + 1, x]


def run_copies(copies):
    for c in copies:
        c.start()
    for c in copies:
        c.wait()


def outer_base(s, images):
    core = lax.rem(s, 2)
    half = images // 2
    k = jnp.where(core == 0, s * images - half, (s + 1) * images)
    return jnp.clip(k, 0, None)


def inner_base(s, images):
    core = lax.rem(s, 2)
    half = images // 2
    return jnp.where(core == 0, (s + 1) * images, s * images - half)


def border_parts(p, r, n):
    return (
        p.at[:, pl.ds(2, 2)],
        r.at[:, pl.ds(1, 4)],
        p.at[:, pl.ds(n - 4, 2)],
        r.at[:, pl.ds(n - 5, 4)],
    )


def inside_a_kernel(
    segs,
    place,
    path,
    from_inner,
    p2,
    p_low,
    r_low,
    p_high,
    r_high,
    p_kept,
    r_kept,
    p,
    r,
    sems,
):
    images, n = path.shape[0], path.shape[1]
    s = place[0]
    core = lax.rem(s, 2)
    run_copies(
        [
            pltpu.make_async_copy(path, p.at[pl.ds(2, images)], sems.at[0]),
            pltpu.make_async_copy(
                from_inner, p.at[pl.ds(jnp.where(core == 0, images + 2, 0), 2)], sems.at[1]
            ),
        ]
    )
    descend(p, r, images, s, segs, inside_ranges(n), inner_rows(images, core), ())
    p_row = jnp.where(core == 0, 2, images)
    r_row = jnp.where(core == 0, 2, images - 1)
    p2_row = jnp.where(core == 0, 2, 0)
    plan = list(zip(border_parts(p, r, n), (p_low, r_low, p_high, r_high))) + [
        (p.at[pl.ds(p_row, 2)], p_kept),
        (r.at[pl.ds(r_row, 2)], r_kept),
        (
            p.at[pl.ds(p2_row + 2, images - 2), pl.ds(4, n - 8)],
            p2.at[pl.ds(p2_row, images - 2)],
        ),
    ]
    run_copies([pltpu.make_async_copy(a, b, sems.at[i]) for i, (a, b) in enumerate(plan)])


def inside_b_kernel(
    segs,
    place,
    offsets,
    weights,
    from_outer,
    p_kept,
    r_kept,
    p2_in,
    p_low_in,
    r_low_in,
    p_high_in,
    r_high_in,
    p2,
    p_low,
    r_low,
    p_high,
    r_high,
    slots,
    p,
    r,
    sems,
):
    del p_low_in, r_low_in, p_high_in, r_high_in
    images, n = p2_in.shape[0], p_kept.shape[1]
    s = place[0]
    core = lax.rem(s, 2)
    p2_row = jnp.where(core == 0, 2, 0)
    done = pltpu.make_async_copy(
        p2_in.at[pl.ds(p2_row, images - 2)],
        p.at[pl.ds(p2_row + 2, images - 2), pl.ds(4, n - 8)],
        sems.at[5],
    )
    done.start()
    run_copies(
        [
            pltpu.make_async_copy(
                from_outer, p.at[pl.ds(jnp.where(core == 0, 0, images + 2), 2)], sems.at[0]
            ),
            pltpu.make_async_copy(
                p_kept, p.at[pl.ds(jnp.where(core == 0, 2, images), 2)], sems.at[1]
            ),
            pltpu.make_async_copy(
                r_kept, r.at[pl.ds(jnp.where(core == 0, 2, images - 1), 2)], sems.at[2]
            ),
        ]
    )
    descend(p, r, images, s, segs, inside_ranges(n), outer_rows(images, core), ())
    done.wait()
    p_rows = pl.ds(jnp.where(core == 0, 0, images), 4)
    r_rows = pl.ds(jnp.where(core == 0, 0, images), 3)
    new_row = jnp.where(core == 0, 0, images - 2)
    parts = border_parts(p, r, n)
    plan = [
        (part.at[rows], out.at[rows])
        for part, out, rows in zip(
            parts, (p_low, r_low, p_high, r_high), (p_rows, r_rows, p_rows, r_rows)
        )
    ] + [(p.at[pl.ds(new_row + 2, 2), pl.ds(4, n - 8)], p2.at[pl.ds(new_row, 2)])]
    copies = [pltpu.make_async_copy(a, b, sems.at[i]) for i, (a, b) in enumerate(plan)]
    for c in copies:
        c.start()
    half = images // 2
    total = segs * images
    k0 = outer_base(s, images)

    def to_slots(i, x):
        k = jnp.minimum(k0 + i, total - 1)
        slots[i, x] = mix(weights, offsets, k, p, 2, x + 4)

    each_plane((0, half), (0, n - 8), to_slots)
    for c in copies:
        c.wait()


def edge_kernel(
    segs,
    tiles,
    low,
    place,
    offsets,
    weights,
    path,
    from_outer,
    from_inner,
    beyond,
    corner_outer,
    corner_inner,
    p_border,
    r_border,
    p2,
    slots,
    p,
    r,
    sems,
):
    images, n = path.shape[0], path.shape[1]
    s, t = place[0], place[1]
    core = lax.rem(s, 2)
    outer_near = jnp.where(core == 0, 1, images + 2)
    outer_far = jnp.where(core == 0, 0, images + 3)
    inner_near = jnp.where(core == 0, images + 2, 1)
    inner_far = jnp.where(core == 0, images + 3, 0)
    outer_row = jnp.where(core == 0, 0, images + 2)
    inner_row = jnp.where(core == 0, images + 2, 0)
    own, at = (pl.ds(0, 2), pl.ds(4, 2)) if low else (pl.ds(n - 2, 2), pl.ds(6, 2))
    three, two = (pl.ds(1, 3), pl.ds(2, 2)) if low else (pl.ds(8, 3), pl.ds(8, 2))
    plan = [
        (path.at[:, own], p.at[pl.ds(2, images), at]),
        (from_outer.at[:, own], p.at[pl.ds(outer_row, 2), at]),
        (from_inner.at[:, own], p.at[pl.ds(inner_row, 2), at]),
        (beyond, p.at[pl.ds(2, images), pl.ds(0 if low else 8, 4)]),
        (corner_outer.at[pl.ds(0, 3)], p.at[outer_near, three]),
        (corner_outer.at[pl.ds(3, 2)], p.at[outer_far, two]),
        (corner_inner.at[pl.ds(0, 3)], p.at[inner_near, three]),
        (corner_inner.at[pl.ds(3, 2)], p.at[inner_far, two]),
        (p_border, p.at[:, pl.ds(6 if low else 4, 2)]),
        (r_border, r.at[:, pl.ds(5 if low else 3, 4)]),
    ]
    run_copies([pltpu.make_async_copy(a, b, sems.at[i]) for i, (a, b) in enumerate(plan)])
    half = images // 2
    total = segs * images
    k0 = outer_base(s, images)
    outside = (t == 0, (1, 4)) if low else (t == tiles - 1, (8, 11))
    ranges = (((1, 5), (2, 6)), ((3, 7), (4, 8)))
    if not low:
        ranges = (((7, 11), (6, 10)), ((5, 9), (4, 8)))
    descend(p, r, images, s, segs, ranges, all_rows(images), (outside,))

    def to_slots(i, x):
        k = jnp.minimum(k0 + i, total - 1)
        slots[i, x] = mix(weights, offsets, k, p, 2, x + 4)

    each_plane((0, half), (0, 4), to_slots)

    def to_p2(j, x):
        p2[j, x] = p[j + 2, x + 4]

    each_plane((0, images), (0, 4), to_p2)


def corner_kernel(low, first_if_zero, place, src, out, sems):
    images, width = src.shape[0], src.shape[1]
    at_first = (lax.rem(place[0], 2) == 0) == first_if_zero
    near = jnp.where(at_first, 0, images - 1)
    far = jnp.where(at_first, 1, images - 2)
    three, two = (pl.ds(0, 3), pl.ds(0, 2)) if low else (pl.ds(width - 3, 3), pl.ds(width - 2, 2))
    run_copies(
        [
            pltpu.make_async_copy(src.at[near, three], out.at[pl.ds(0, 3)], sems.at[0]),
            pltpu.make_async_copy(src.at[far, two], out.at[pl.ds(3, 2)], sems.at[1]),
        ]
    )


def pair_kernel(first_if_zero, place, path, out, sems):
    images = path.shape[0]
    at_first = (lax.rem(place[0], 2) == 0) == first_if_zero
    first = jnp.where(at_first, 0, images - 2)
    run_copies([pltpu.make_async_copy(path.at[pl.ds(first, 2)], out, sems.at[0])])


def plane_parts(n):
    return ((0, 4, 0), (4, n - 4, 1), (n - 4, n, 2))


def inner_slots_kernel(place, offsets, weights, low, inside, high, slots):
    images, n = inside.shape[0], slots.shape[1]
    half = images // 2
    k0 = inner_base(place[0], images)
    for lo, hi, which in plane_parts(n):
        p = (low, inside, high)[which]

        def body(i, x):
            slots[i, x + lo] = mix(weights, offsets, k0 + i, p, 0, x)

        each_plane((0, half), (0, hi - lo), body)


def own_kernel(place, offsets, weights, low, inside, high, out):
    images, n = out.shape[0], out.shape[1]
    k0 = place[0] * images
    for lo, hi, which in plane_parts(n):
        p = (low, inside, high)[which]

        def body(i, x):
            out[i, x + lo] = mix(weights, offsets, k0 + i, p, 0, x)

        each_plane((0, images), (0, hi - lo), body)


def source_step(counts, k, s, segs):
    end = jnp.int32(0)
    source = jnp.int32(0)
    for i in range(segs):
        end = end + counts[i]
        source = source + jnp.where(end <= k, 1, 0)
    return source - s


def place_kernel(segs, place, counts, low, inside, high, inner_part, own, out, sems):
    del own
    images, n = out.shape[0], out.shape[1]
    half = images // 2
    s = place[0]
    core = lax.rem(s, 2)

    def copies(i, slot, from_outer):
        for lo, hi, which in plane_parts(n):
            if from_outer:
                src = (low, inside, high)[which].at[slot]
            else:
                src = inner_part.at[slot, pl.ds(lo, hi - lo)]
            yield pltpu.make_async_copy(src, out.at[i, pl.ds(lo, hi - lo)], sems.at[i, which])

    for start in (True, False):
        for i in range(images):
            step = source_step(counts, s * images + i, s, segs)
            slot = i % half
            foreign = (step < 0) if i < half else (step > 0)
            outer_core = 0 if i < half else 1

            for from_outer in (True, False):

                @pl.when(foreign & ((core == outer_core) == from_outer))
                def _(i=i, slot=slot, from_outer=from_outer):
                    for c in copies(i, slot, from_outer):
                        if start:
                            c.start()
                        else:
                            c.wait()


def field(*shape):
    return jax.ShapeDtypeStruct(shape, jnp.float32)


def cost(planes, arrays):
    return pl.CostEstimate(
        flops=planes * 8192 * 60, bytes_accessed=arrays * 2**20, transcendentals=0
    )


def params(mib):
    return pltpu.CompilerParams(vmem_limit_bytes=mib * 2**20)


def step(path_field, counts, offsets, weights):
    images, n, gy, gz = path_field.shape
    segs, tiles = lax.axis_size("seg"), lax.axis_size("tile")
    s, t = lax.axis_index("seg"), lax.axis_index("tile")
    half = images // 2
    place = jnp.stack([s, t]).astype(jnp.int32)

    def send(block, ds_of, dt):
        return lax.ppermute(block, AXES, routes(segs, tiles, ds_of, dt))

    def stay(_):
        return 0

    def call(kernel, *args, **settings):
        return pl.pallas_call(kernel, **settings)(*args)

    def corner(array, low, first_if_zero):
        return call(
            functools.partial(corner_kernel, low, first_if_zero),
            place,
            array,
            out_shape=field(5, gy, gz),
            in_specs=[SMEM, ANY],
            out_specs=VMEM,
            scratch_shapes=[pltpu.SemaphoreType.DMA((2,))],
            compiler_params=params(1),
            cost_estimate=cost(0, 1),
        )

    def pair(first_if_zero):
        return call(
            functools.partial(pair_kernel, first_if_zero),
            place,
            path_field,
            out_shape=field(2, n, gy, gz),
            in_specs=[SMEM, ANY],
            out_specs=VMEM,
            scratch_shapes=[pltpu.SemaphoreType.DMA((1,))],
            compiler_params=params(2),
            cost_estimate=cost(0, 2),
        )

    from_outer = send(pair(True), outer, 0)
    from_inner = send(pair(False), inner, 0)
    below = send(path_field[:, n - 4 :], stay, 1)
    above = send(path_field[:, :4], stay, -1)
    corner_below = send(corner(path_field, False, True), outer, 1)
    corner_above = send(corner(path_field, True, True), outer, -1)

    border = (field(images + 4, 2, gy, gz), field(images + 3, 4, gy, gz))
    levels = [
        pltpu.VMEM((images + 4, n, gy, gz), jnp.float32),
        pltpu.VMEM((images + 3, n, gy, gz), jnp.float32),
        pltpu.SemaphoreType.DMA((7,)),
    ]
    *first, p_kept, r_kept = call(
        functools.partial(inside_a_kernel, segs),
        place,
        path_field,
        from_inner,
        out_shape=(field(images, n - 8, gy, gz),)
        + border * 2
        + (field(2, n, gy, gz), field(2, n, gy, gz)),
        in_specs=[SMEM, ANY, ANY],
        out_specs=(ANY,) * 7,
        scratch_shapes=levels,
        compiler_params=params(14),
        cost_estimate=cost(36 * 10, 8),
    )
    p2_inside, *borders, slots_inside = call(
        functools.partial(inside_b_kernel, segs),
        place,
        offsets,
        weights,
        from_outer,
        p_kept,
        r_kept,
        *first,
        out_shape=(field(images, n - 8, gy, gz),) + border * 2 + (field(half, n - 8, gy, gz),),
        in_specs=[SMEM, SMEM, SMEM] + [ANY] * 8,
        out_specs=(ANY,) * 5 + (VMEM,),
        input_output_aliases={6 + i: i for i in range(5)},
        scratch_shapes=levels,
        compiler_params=params(14),
        cost_estimate=cost(9 * 10, 6),
    )
    got_inside = send(slots_inside, outer, 0)

    def edge(low, beyond, corner_outer):
        corner_inner = send(corner(beyond, not low, False), inner, 0)
        return call(
            functools.partial(edge_kernel, segs, tiles, low),
            place,
            offsets,
            weights,
            path_field,
            from_outer,
            from_inner,
            beyond,
            corner_outer,
            corner_inner,
            *(borders[:2] if low else borders[2:]),
            out_shape=(field(images, 4, gy, gz), field(half, 4, gy, gz)),
            in_specs=[SMEM, SMEM, SMEM] + [ANY] * 8,
            out_specs=(VMEM, VMEM),
            scratch_shapes=[
                pltpu.VMEM((images + 4, 12, gy, gz), jnp.float32),
                pltpu.VMEM((images + 3, 12, gy, gz), jnp.float32),
                pltpu.SemaphoreType.DMA((10,)),
            ],
            compiler_params=params(14),
            cost_estimate=cost(28 * 10, 6),
        )

    p2_low, slots_low = edge(True, below, corner_below)
    got_low = send(slots_low, outer, 0)
    p2_high, slots_high = edge(False, above, corner_above)
    got_high = send(slots_high, outer, 0)

    slots_inner = call(
        inner_slots_kernel,
        place,
        offsets,
        weights,
        p2_low,
        p2_inside,
        p2_high,
        out_shape=field(half, n, gy, gz),
        in_specs=[SMEM, SMEM, SMEM, VMEM, VMEM, VMEM],
        out_specs=VMEM,
        compiler_params=params(8),
        cost_estimate=cost(16, 6),
    )
    got_inner = send(slots_inner, inner, 0)
    own = call(
        own_kernel,
        place,
        offsets,
        weights,
        p2_low,
        p2_inside,
        p2_high,
        out_shape=field(images, n, gy, gz),
        in_specs=[SMEM, SMEM, SMEM, VMEM, VMEM, VMEM],
        out_specs=VMEM,
        compiler_params=params(10),
        cost_estimate=cost(32, 8),
    )
    return call(
        functools.partial(place_kernel, segs),
        place,
        counts,
        got_low,
        got_inside,
        got_high,
        got_inner,
        own,
        out_shape=field(images, n, gy, gz),
        in_specs=[SMEM, SMEM, VMEM, VMEM, VMEM, VMEM, ANY],
        out_specs=ANY,
        scratch_shapes=[pltpu.SemaphoreType.DMA((images, 3))],
        input_output_aliases={6: 0},
        compiler_params=params(6),
        cost_estimate=cost(2, 4),
    )


def solution(mesh):
    return jax.shard_map(
        step,
        mesh=mesh,
        in_specs=(P("seg", "tile", None, None), P(), P(), P()),
        out_specs=P("seg", "tile", None, None),
        check_vma=False,
    )
```

```python
import functools

import jax
import jax.numpy as jnp
from jax import lax
from jax.experimental import pallas as pl
from jax.experimental.pallas import tpu as pltpu
from jax.sharding import PartitionSpec as P


KAPPA_COEF = 1.0
TIME_STEP = 0.1
DESCENT_RATE = 0.01


AXES = ("seg", "tile")
BODY_PLANES = 16
ANY = pl.BlockSpec(memory_space=pl.ANY)
VMEM = pl.BlockSpec(memory_space=pltpu.VMEM)
SMEM = pl.BlockSpec(memory_space=pltpu.SMEM)


def routes(segs, tiles, ds_of, dt_of):
    pairs = []
    for s in range(segs):
        if ds_of(s) is None:
            continue
        for t in range(tiles):
            to_s, to_t = s + ds_of(s), t + dt_of(t)
            if 0 <= to_s < segs and 0 <= to_t < tiles:
                pairs.append((s * tiles + t, to_s * tiles + to_t))
    return pairs


def outer(s):
    return 1 if s % 2 else -1


def along_y(s):
    return outer(s) if s % 4 in (0, 3) else None


def along_z(s):
    return outer(s) if s % 4 in (1, 2) else None


def inner(s):
    return -1 if s % 2 else 1


def neighbour_sum(ref, j, x, c):
    total = ref[j, x + 1] + ref[j, x - 1]
    for axis in (0, 1):
        total = total + (pltpu.roll(c, 1, axis) + pltpu.roll(c, c.shape[axis] - 1, axis))
    return total


def each_plane(images, planes, body):
    first, count = images
    width = planes[1] - planes[0]
    group = max(1, min(count, BODY_PLANES // width))

    def rows(start, size):
        for j in range(size):
            for x in range(*planes):
                body(start + j, x)

    def over_groups(i, carry):
        rows(first + i * group, group)
        return carry

    lax.fori_loop(0, count // group, over_groups, 0)
    if count % group:
        rows(first + count - count % group, count % group)


def residual_stage(p, r, images, planes):
    def body(j, x):
        c = p[j, x]
        linear = 6.0 * KAPPA_COEF - 1.0 - 1.0 / TIME_STEP
        total = neighbour_sum(p, j, x, c)
        if KAPPA_COEF != 1.0:
            total = KAPPA_COEF * total
        r[j, x] = p[j + 1, x] * (1.0 / TIME_STEP) - total + c * (c * c + linear)

    each_plane(images, planes, body)


def update_stage(p, r, images, planes, first_id, last_id):
    def body(j, x):
        c = p[j, x]
        rc = r[j, x]
        linear = 1.0 + TIME_STEP * (1.0 - 6.0 * KAPPA_COEF)
        pull = rc * (linear - (3.0 * TIME_STEP) * (c * c)) - r[j - 1, x]
        down = (TIME_STEP * KAPPA_COEF) * neighbour_sum(r, j, x, rc) + pull
        image_id = first_id + j
        rate = jnp.where((image_id > 0) & (image_id < last_id), DESCENT_RATE, 0.0)
        p[j, x] = c + rate * down

    each_plane(images, planes, body)


def clear(ref, images, planes):
    def body(j, x):
        ref[j, x] = jnp.zeros(ref.shape[2:], ref.dtype)

    each_plane(images, planes, body)


def descend(p, r, images, s, segs, ranges, rows, outside):
    first_id, last_id = s * images - 2, segs * images - 1
    for step in range(2):
        at, moved = ranges[step]
        residual_rows, update_rows = rows[step]
        residual_stage(p, r, residual_rows, at)

        @pl.when(s == 0)
        def _():
            clear(r, (step, 2 - step), at)

        @pl.when(s == segs - 1)
        def _():
            clear(r, (images + 1, 2 - step), at)

        for cond, planes in outside:

            @pl.when(cond)
            def _(planes=planes):
                clear(r, residual_rows, planes)

        update_stage(p, r, update_rows, moved, first_id, last_id)
        if step == 0:
            for cond, planes in outside:

                @pl.when(cond)
                def _(planes=planes):
                    clear(p, update_rows, planes)


def all_rows(images):
    return (
        ((0, images + 3), (1, images + 2)),
        ((1, images + 1), (2, images)),
    )


def inner_rows(images, core):
    a = jnp.where(core == 0, 2, 0)
    return (
        ((a, images + 1), (a + 1, images)),
        ((a + 1, images - 1), (a + 2, images - 2)),
    )


def outer_rows(images, core):
    starts = [jnp.where(core == 0, a, images + b) for a, b in ((0, 1), (1, 1), (1, 0), (2, 0))]
    first, second, third, fourth = [(a, 2) for a in starts]
    return ((first, second), (third, fourth))


def inside_ranges(n):
    return (((1, n - 1), (2, n - 2)), ((3, n - 3), (4, n - 4)))


def mix(weights, offsets, k, p, base, x):
    w = weights[k]
    q = offsets[k] + base
    return w * p[q, x] + (1.0 - w) * p[q + 1, x]


def run_copies(copies):
    for c in copies:
        c.start()
    for c in copies:
        c.wait()


def outer_base(s, images):
    core = lax.rem(s, 2)
    half = images // 2
    k = jnp.where(core == 0, s * images - half, (s + 1) * images)
    return jnp.clip(k, 0, None)


def inner_base(s, images):
    core = lax.rem(s, 2)
    half = images // 2
    return jnp.where(core == 0, (s + 1) * images, s * images - half)


def border_parts(p, r, n):
    return (
        p.at[:, pl.ds(2, 2)],
        r.at[:, pl.ds(1, 4)],
        p.at[:, pl.ds(n - 4, 2)],
        r.at[:, pl.ds(n - 5, 4)],
    )


def inside_a_kernel(
    segs,
    place,
    path,
    from_inner,
    p2,
    p_low,
    r_low,
    p_high,
    r_high,
    p_kept,
    r_kept,
    p,
    r,
    sems,
):
    images, n = path.shape[0], path.shape[1]
    s = place[0]
    core = lax.rem(s, 2)
    run_copies(
        [
            pltpu.make_async_copy(path, p.at[pl.ds(2, images)], sems.at[0]),
            pltpu.make_async_copy(
                from_inner, p.at[pl.ds(jnp.where(core == 0, images + 2, 0), 2)], sems.at[1]
            ),
        ]
    )
    descend(p, r, images, s, segs, inside_ranges(n), inner_rows(images, core), ())
    p_row = jnp.where(core == 0, 2, images)
    r_row = jnp.where(core == 0, 2, images - 1)
    p2_row = jnp.where(core == 0, 2, 0)
    plan = list(zip(border_parts(p, r, n), (p_low, r_low, p_high, r_high))) + [
        (p.at[pl.ds(p_row, 2)], p_kept),
        (r.at[pl.ds(r_row, 2)], r_kept),
        (
            p.at[pl.ds(p2_row + 2, images - 2), pl.ds(4, n - 8)],
            p2.at[pl.ds(p2_row, images - 2)],
        ),
    ]
    run_copies([pltpu.make_async_copy(a, b, sems.at[i]) for i, (a, b) in enumerate(plan)])


def inside_b_kernel(
    segs,
    place,
    offsets,
    weights,
    from_outer,
    p_kept,
    r_kept,
    p2_in,
    p_low_in,
    r_low_in,
    p_high_in,
    r_high_in,
    p2,
    p_low,
    r_low,
    p_high,
    r_high,
    slots_near,
    slots_far,
    p,
    r,
    sems,
):
    del p_low_in, r_low_in, p_high_in, r_high_in
    images, n = p2_in.shape[0], p_kept.shape[1]
    s = place[0]
    core = lax.rem(s, 2)
    p2_row = jnp.where(core == 0, 2, 0)
    done = pltpu.make_async_copy(
        p2_in.at[pl.ds(p2_row, images - 2)],
        p.at[pl.ds(p2_row + 2, images - 2), pl.ds(4, n - 8)],
        sems.at[5],
    )
    done.start()
    run_copies(
        [
            pltpu.make_async_copy(
                from_outer, p.at[pl.ds(jnp.where(core == 0, 0, images + 2), 2)], sems.at[0]
            ),
            pltpu.make_async_copy(
                p_kept, p.at[pl.ds(jnp.where(core == 0, 2, images), 2)], sems.at[1]
            ),
            pltpu.make_async_copy(
                r_kept, r.at[pl.ds(jnp.where(core == 0, 2, images - 1), 2)], sems.at[2]
            ),
        ]
    )
    descend(p, r, images, s, segs, inside_ranges(n), outer_rows(images, core), ())
    done.wait()
    p_rows = pl.ds(jnp.where(core == 0, 0, images), 4)
    r_rows = pl.ds(jnp.where(core == 0, 0, images), 3)
    new_row = jnp.where(core == 0, 0, images - 2)
    parts = border_parts(p, r, n)
    plan = [
        (part.at[rows], out.at[rows])
        for part, out, rows in zip(
            parts, (p_low, r_low, p_high, r_high), (p_rows, r_rows, p_rows, r_rows)
        )
    ] + [(p.at[pl.ds(new_row + 2, 2), pl.ds(4, n - 8)], p2.at[pl.ds(new_row, 2)])]
    copies = [pltpu.make_async_copy(a, b, sems.at[i]) for i, (a, b) in enumerate(plan)]
    for c in copies:
        c.start()
    quarter = images // 4
    total = segs * images
    for slots, k0 in (
        (slots_near, outer_base(s, images)),
        (slots_far, outer_base(s, images) + quarter),
    ):

        def to_slots(i, x, slots=slots, k0=k0):
            k = jnp.minimum(k0 + i, total - 1)
            slots[i, x] = mix(weights, offsets, k, p, 2, x + 4)

        each_plane((0, quarter), (0, n - 8), to_slots)
    for c in copies:
        c.wait()


def edge_kernel(
    segs,
    tiles,
    low,
    place,
    offsets,
    weights,
    path,
    from_outer,
    from_inner,
    beyond,
    corner_outer,
    corner_inner,
    p_border,
    r_border,
    p2,
    slots,
    p,
    r,
    sems,
):
    images, n = path.shape[0], path.shape[1]
    s, t = place[0], place[1]
    core = lax.rem(s, 2)
    outer_near = jnp.where(core == 0, 1, images + 2)
    outer_far = jnp.where(core == 0, 0, images + 3)
    inner_near = jnp.where(core == 0, images + 2, 1)
    inner_far = jnp.where(core == 0, images + 3, 0)
    outer_row = jnp.where(core == 0, 0, images + 2)
    inner_row = jnp.where(core == 0, images + 2, 0)
    own, at = (pl.ds(0, 2), pl.ds(4, 2)) if low else (pl.ds(n - 2, 2), pl.ds(6, 2))
    three, two = (pl.ds(1, 3), pl.ds(2, 2)) if low else (pl.ds(8, 3), pl.ds(8, 2))
    plan = [
        (path.at[:, own], p.at[pl.ds(2, images), at]),
        (from_outer.at[:, own], p.at[pl.ds(outer_row, 2), at]),
        (from_inner.at[:, own], p.at[pl.ds(inner_row, 2), at]),
        (beyond, p.at[pl.ds(2, images), pl.ds(0 if low else 8, 4)]),
        (corner_outer.at[pl.ds(0, 3)], p.at[outer_near, three]),
        (corner_outer.at[pl.ds(3, 2)], p.at[outer_far, two]),
        (corner_inner.at[pl.ds(0, 3)], p.at[inner_near, three]),
        (corner_inner.at[pl.ds(3, 2)], p.at[inner_far, two]),
        (p_border, p.at[:, pl.ds(6 if low else 4, 2)]),
        (r_border, r.at[:, pl.ds(5 if low else 3, 4)]),
    ]
    run_copies([pltpu.make_async_copy(a, b, sems.at[i]) for i, (a, b) in enumerate(plan)])
    half = images // 2
    total = segs * images
    k0 = outer_base(s, images)
    outside = (t == 0, (1, 4)) if low else (t == tiles - 1, (8, 11))
    ranges = (((1, 5), (2, 6)), ((3, 7), (4, 8)))
    if not low:
        ranges = (((7, 11), (6, 10)), ((5, 9), (4, 8)))
    descend(p, r, images, s, segs, ranges, all_rows(images), (outside,))

    def to_slots(i, x):
        k = jnp.minimum(k0 + i, total - 1)
        slots[i, x] = mix(weights, offsets, k, p, 2, x + 4)

    each_plane((0, half), (0, 4), to_slots)

    def to_p2(j, x):
        p2[j, x] = p[j + 2, x + 4]

    each_plane((0, images), (0, 4), to_p2)


def corner_kernel(low, first_if_zero, place, src, out, sems):
    images, width = src.shape[0], src.shape[1]
    at_first = (lax.rem(place[0], 2) == 0) == first_if_zero
    near = jnp.where(at_first, 0, images - 1)
    far = jnp.where(at_first, 1, images - 2)
    three, two = (pl.ds(0, 3), pl.ds(0, 2)) if low else (pl.ds(width - 3, 3), pl.ds(width - 2, 2))
    run_copies(
        [
            pltpu.make_async_copy(src.at[near, three], out.at[pl.ds(0, 3)], sems.at[0]),
            pltpu.make_async_copy(src.at[far, two], out.at[pl.ds(3, 2)], sems.at[1]),
        ]
    )


def pair_kernel(first_if_zero, place, path, out, sems):
    images = path.shape[0]
    at_first = (lax.rem(place[0], 2) == 0) == first_if_zero
    first = jnp.where(at_first, 0, images - 2)
    run_copies([pltpu.make_async_copy(path.at[pl.ds(first, 2)], out, sems.at[0])])


def plane_parts(n):
    return ((0, 4, 0), (4, n - 4, 1), (n - 4, n, 2))


def inner_slots_kernel(place, offsets, weights, low, inside, high, slots):
    images, n = inside.shape[0], slots.shape[1]
    half = images // 2
    k0 = inner_base(place[0], images)
    for lo, hi, which in plane_parts(n):
        p = (low, inside, high)[which]

        def body(i, x):
            slots[i, x + lo] = mix(weights, offsets, k0 + i, p, 0, x)

        each_plane((0, half), (0, hi - lo), body)


def own_kernel(place, offsets, weights, low, inside, high, out):
    images, n = out.shape[0], out.shape[1]
    k0 = place[0] * images
    for lo, hi, which in plane_parts(n):
        p = (low, inside, high)[which]

        def body(i, x):
            out[i, x + lo] = mix(weights, offsets, k0 + i, p, 0, x)

        each_plane((0, images), (0, hi - lo), body)


def bounds(segs, counts, s):
    before = jnp.int32(0)
    end = jnp.int32(0)
    for i in range(segs):
        before = before + jnp.where(i < s, counts[i], 0)
        end = end + jnp.where(i <= s, counts[i], 0)
    return before, end


def choose_kernel(segs, place, counts, near, lent, out, sems):
    s = place[0]
    images = 4 * near.shape[0]
    before, end = bounds(segs, counts, s)
    gives = jnp.where(lax.rem(s, 2) == 0, before < s * images, end > (s + 1) * images)
    gives = gives | (lax.rem(lax.div(s + 1, 2), 2) == 1)

    @pl.when(gives)
    def _():
        run_copies([pltpu.make_async_copy(near, out, sems.at[0])])

    @pl.when(jnp.logical_not(gives))
    def _():
        run_copies([pltpu.make_async_copy(lent, out, sems.at[0])])


def place_kernel(
    segs, place, counts, low, near, far, back, high, inner_part, own, out, sems
):
    del own
    images, n = out.shape[0], out.shape[1]
    half = images // 2
    quarter = half // 2
    s = place[0]
    core = lax.rem(s, 2)
    before, end = bounds(segs, counts, s)
    is_z = lax.rem(lax.div(s + 1, 2), 2) == 1

    def copies(i, slot, from_outer, rest):
        for lo, hi, which in plane_parts(n):
            if from_outer:
                inside = near if slot < quarter else rest
                row = slot if which != 1 else slot % quarter
                src = (low, inside, high)[which].at[row]
            else:
                src = inner_part.at[slot, pl.ds(lo, hi - lo)]
            yield pltpu.make_async_copy(src, out.at[i, pl.ds(lo, hi - lo)], sems.at[i, which])

    for start in (True, False):
        for i in range(images):
            k = s * images + i
            slot = i % half
            foreign = (k < before) if i < half else (k >= end)
            outer_core = 0 if i < half else 1

            cases = [((core == outer_core) & is_z, True, far)]
            cases += [((core == outer_core) & jnp.logical_not(is_z), True, back)]
            cases += [(core != outer_core, False, None)]
            for cond, from_outer, rest in cases:

                @pl.when(foreign & cond)
                def _(i=i, slot=slot, from_outer=from_outer, rest=rest):
                    for c in copies(i, slot, from_outer, rest):
                        if start:
                            c.start()
                        else:
                            c.wait()


def field(*shape):
    return jax.ShapeDtypeStruct(shape, jnp.float32)


def cost(planes, arrays):
    return pl.CostEstimate(
        flops=planes * 8192 * 60, bytes_accessed=arrays * 2**20, transcendentals=0
    )


def params(mib):
    return pltpu.CompilerParams(vmem_limit_bytes=mib * 2**20)


def step(path_field, counts, offsets, weights):
    images, n, gy, gz = path_field.shape
    segs, tiles = lax.axis_size("seg"), lax.axis_size("tile")
    s, t = lax.axis_index("seg"), lax.axis_index("tile")
    half = images // 2
    place = jnp.stack([s, t]).astype(jnp.int32)

    def send(block, ds_of, dt):
        dt_of = dt if callable(dt) else lambda _: dt
        return lax.ppermute(block, AXES, routes(segs, tiles, ds_of, dt_of))

    def across(tile):
        return -1 if tile % 2 else 1

    def stay(_):
        return 0

    def call(kernel, *args, **settings):
        return pl.pallas_call(kernel, **settings)(*args)

    def corner(array, low, first_if_zero):
        return call(
            functools.partial(corner_kernel, low, first_if_zero),
            place,
            array,
            out_shape=field(5, gy, gz),
            in_specs=[SMEM, ANY],
            out_specs=VMEM,
            scratch_shapes=[pltpu.SemaphoreType.DMA((2,))],
            compiler_params=params(1),
            cost_estimate=cost(0, 1),
        )

    def pair(first_if_zero):
        return call(
            functools.partial(pair_kernel, first_if_zero),
            place,
            path_field,
            out_shape=field(2, n, gy, gz),
            in_specs=[SMEM, ANY],
            out_specs=VMEM,
            scratch_shapes=[pltpu.SemaphoreType.DMA((1,))],
            compiler_params=params(2),
            cost_estimate=cost(0, 2),
        )

    from_outer = send(pair(True), outer, 0)
    from_inner = send(pair(False), inner, 0)
    below = send(path_field[:, n - 4 :], stay, 1)
    above = send(path_field[:, :4], stay, -1)
    corner_below = send(corner(path_field, False, True), outer, 1)
    corner_above = send(corner(path_field, True, True), outer, -1)

    border = (field(images + 4, 2, gy, gz), field(images + 3, 4, gy, gz))
    levels = [
        pltpu.VMEM((images + 4, n, gy, gz), jnp.float32),
        pltpu.VMEM((images + 3, n, gy, gz), jnp.float32),
        pltpu.SemaphoreType.DMA((7,)),
    ]
    *first, p_kept, r_kept = call(
        functools.partial(inside_a_kernel, segs),
        place,
        path_field,
        from_inner,
        out_shape=(field(images, n - 8, gy, gz),)
        + border * 2
        + (field(2, n, gy, gz), field(2, n, gy, gz)),
        in_specs=[SMEM, ANY, ANY],
        out_specs=(ANY,) * 7,
        scratch_shapes=levels,
        compiler_params=params(14),
        cost_estimate=cost(36 * 10, 8),
    )
    p2_inside, *borders, slots_near, slots_far = call(
        functools.partial(inside_b_kernel, segs),
        place,
        offsets,
        weights,
        from_outer,
        p_kept,
        r_kept,
        *first,
        out_shape=(field(images, n - 8, gy, gz),) + border * 2 + (field(half // 2, n - 8, gy, gz),) * 2,
        in_specs=[SMEM, SMEM, SMEM] + [ANY] * 8,
        out_specs=(ANY,) * 5 + (VMEM,) * 2,
        input_output_aliases={6 + i: i for i in range(5)},
        scratch_shapes=levels,
        compiler_params=params(14),
        cost_estimate=cost(9 * 10, 6),
    )
    lent = send(slots_far, along_y, across)
    chosen = call(
        functools.partial(choose_kernel, segs),
        place,
        counts,
        slots_near,
        lent,
        out_shape=field(half // 2, n - 8, gy, gz),
        in_specs=[SMEM, SMEM, ANY, ANY],
        out_specs=VMEM,
        scratch_shapes=[pltpu.SemaphoreType.DMA((1,))],
        compiler_params=params(1),
        cost_estimate=cost(0, 1),
    )
    got_near = send(chosen, outer, 0)
    got_far = send(slots_far, along_z, 0)
    got_back = send(got_near, along_y, across)

    def edge(low, beyond, corner_outer):
        corner_inner = send(corner(beyond, not low, False), inner, 0)
        return call(
            functools.partial(edge_kernel, segs, tiles, low),
            place,
            offsets,
            weights,
            path_field,
            from_outer,
            from_inner,
            beyond,
            corner_outer,
            corner_inner,
            *(borders[:2] if low else borders[2:]),
            out_shape=(field(images, 4, gy, gz), field(half, 4, gy, gz)),
            in_specs=[SMEM, SMEM, SMEM] + [ANY] * 8,
            out_specs=(VMEM, VMEM),
            scratch_shapes=[
                pltpu.VMEM((images + 4, 12, gy, gz), jnp.float32),
                pltpu.VMEM((images + 3, 12, gy, gz), jnp.float32),
                pltpu.SemaphoreType.DMA((10,)),
            ],
            compiler_params=params(14),
            cost_estimate=cost(28 * 10, 6),
        )

    p2_low, slots_low = edge(True, below, corner_below)
    got_low = send(slots_low, outer, 0)
    p2_high, slots_high = edge(False, above, corner_above)
    got_high = send(slots_high, outer, 0)

    slots_inner = call(
        inner_slots_kernel,
        place,
        offsets,
        weights,
        p2_low,
        p2_inside,
        p2_high,
        out_shape=field(half, n, gy, gz),
        in_specs=[SMEM, SMEM, SMEM, VMEM, VMEM, VMEM],
        out_specs=VMEM,
        compiler_params=params(8),
        cost_estimate=cost(16, 6),
    )
    got_inner = send(slots_inner, inner, 0)
    own = call(
        own_kernel,
        place,
        offsets,
        weights,
        p2_low,
        p2_inside,
        p2_high,
        out_shape=field(images, n, gy, gz),
        in_specs=[SMEM, SMEM, SMEM, VMEM, VMEM, VMEM],
        out_specs=VMEM,
        compiler_params=params(10),
        cost_estimate=cost(32, 8),
    )
    return call(
        functools.partial(place_kernel, segs),
        place,
        counts,
        got_low,
        got_near,
        got_far,
        got_back,
        got_high,
        got_inner,
        own,
        out_shape=field(images, n, gy, gz),
        in_specs=[SMEM, SMEM] + [VMEM] * 6 + [ANY],
        out_specs=ANY,
        scratch_shapes=[pltpu.SemaphoreType.DMA((images, 3))],
        input_output_aliases={8: 0},
        compiler_params=params(6),
        cost_estimate=cost(2, 4),
    )


def solution(mesh):
    return jax.shard_map(
        step,
        mesh=mesh,
        in_specs=(P("seg", "tile", None, None), P(), P(), P()),
        out_specs=P("seg", "tile", None, None),
        check_vma=False,
    )
```

```python
import functools

import jax
import jax.numpy as jnp
from jax import lax
from jax.experimental import pallas as pl
from jax.experimental.pallas import tpu as pltpu
from jax.sharding import PartitionSpec as P


KAPPA_COEF = 1.0
TIME_STEP = 0.1
DESCENT_RATE = 0.01


AXES = ("seg", "tile")
BODY_PLANES = 16
ANY = pl.BlockSpec(memory_space=pl.ANY)
VMEM = pl.BlockSpec(memory_space=pltpu.VMEM)
SMEM = pl.BlockSpec(memory_space=pltpu.SMEM)


def routes(segs, tiles, ds_of, dt_of):
    pairs = []
    for s in range(segs):
        if ds_of(s) is None:
            continue
        for t in range(tiles):
            to_s, to_t = s + ds_of(s), t + dt_of(t)
            if 0 <= to_s < segs and 0 <= to_t < tiles:
                pairs.append((s * tiles + t, to_s * tiles + to_t))
    return pairs


def outer(s):
    return 1 if s % 2 else -1


def along_y(s):
    return outer(s) if s % 4 in (0, 3) else None


def along_z(s):
    return outer(s) if s % 4 in (1, 2) else None


def inner(s):
    return -1 if s % 2 else 1


def neighbour_sum(ref, j, x, c):
    total = ref[j, x + 1] + ref[j, x - 1]
    for axis in (0, 1):
        total = total + (pltpu.roll(c, 1, axis) + pltpu.roll(c, c.shape[axis] - 1, axis))
    return total


def each_plane(images, planes, body):
    first, count = images
    width = planes[1] - planes[0]
    group = max(1, min(count, BODY_PLANES // width))

    def rows(start, size):
        for j in range(size):
            for x in range(*planes):
                body(start + j, x)

    def over_groups(i, carry):
        rows(first + i * group, group)
        return carry

    lax.fori_loop(0, count // group, over_groups, 0)
    if count % group:
        rows(first + count - count % group, count % group)


def residual_stage(p, r, images, planes):
    def body(j, x):
        c = p[j, x]
        linear = 6.0 * KAPPA_COEF - 1.0 - 1.0 / TIME_STEP
        total = neighbour_sum(p, j, x, c)
        if KAPPA_COEF != 1.0:
            total = KAPPA_COEF * total
        r[j, x] = p[j + 1, x] * (1.0 / TIME_STEP) - total + c * (c * c + linear)

    each_plane(images, planes, body)


def update_stage(p, r, images, planes, first_id, last_id):
    def body(j, x):
        c = p[j, x]
        rc = r[j, x]
        linear = 1.0 + TIME_STEP * (1.0 - 6.0 * KAPPA_COEF)
        pull = rc * (linear - (3.0 * TIME_STEP) * (c * c)) - r[j - 1, x]
        down = (TIME_STEP * KAPPA_COEF) * neighbour_sum(r, j, x, rc) + pull
        image_id = first_id + j
        rate = jnp.where((image_id > 0) & (image_id < last_id), DESCENT_RATE, 0.0)
        p[j, x] = c + rate * down

    each_plane(images, planes, body)


def clear(ref, images, planes):
    def body(j, x):
        ref[j, x] = jnp.zeros(ref.shape[2:], ref.dtype)

    each_plane(images, planes, body)


def descend(p, r, images, s, segs, ranges, rows, outside):
    first_id, last_id = s * images - 2, segs * images - 1
    for step in range(2):
        at, moved = ranges[step]
        residual_rows, update_rows = rows[step]
        residual_stage(p, r, residual_rows, at)

        @pl.when(s == 0)
        def _():
            clear(r, (step, 2 - step), at)

        @pl.when(s == segs - 1)
        def _():
            clear(r, (images + 1, 2 - step), at)

        for cond, planes in outside:

            @pl.when(cond)
            def _(planes=planes):
                clear(r, residual_rows, planes)

        update_stage(p, r, update_rows, moved, first_id, last_id)
        if step == 0:
            for cond, planes in outside:

                @pl.when(cond)
                def _(planes=planes):
                    clear(p, update_rows, planes)


def all_rows(images):
    return (
        ((0, images + 3), (1, images + 2)),
        ((1, images + 1), (2, images)),
    )


def inner_rows(images, core):
    a = jnp.where(core == 0, 2, 0)
    return (
        ((a, images + 1), (a + 1, images)),
        ((a + 1, images - 1), (a + 2, images - 2)),
    )


def outer_rows(images, core):
    starts = [jnp.where(core == 0, a, images + b) for a, b in ((0, 1), (1, 1), (1, 0), (2, 0))]
    first, second, third, fourth = [(a, 2) for a in starts]
    return ((first, second), (third, fourth))


def inside_ranges(n):
    return (((1, n - 1), (2, n - 2)), ((3, n - 3), (4, n - 4)))


def mix(weights, offsets, k, p, base, x):
    w = weights[k]
    q = offsets[k] + base
    return w * p[q, x] + (1.0 - w) * p[q + 1, x]


def run_copies(copies):
    for c in copies:
        c.start()
    for c in copies:
        c.wait()


def outer_base(s, images):
    core = lax.rem(s, 2)
    half = images // 2
    k = jnp.where(core == 0, s * images - half, (s + 1) * images)
    return jnp.clip(k, 0, None)


def inner_base(s, images):
    core = lax.rem(s, 2)
    half = images // 2
    return jnp.where(core == 0, (s + 1) * images, s * images - half)


def border_parts(p, r, n):
    return (
        p.at[:, pl.ds(2, 2)],
        r.at[:, pl.ds(1, 4)],
        p.at[:, pl.ds(n - 4, 2)],
        r.at[:, pl.ds(n - 5, 4)],
    )


def inside_a_kernel(
    segs,
    place,
    path,
    from_inner,
    p2,
    p_low,
    r_low,
    p_high,
    r_high,
    p_kept,
    r_kept,
    p,
    r,
    sems,
):
    images, n = path.shape[0], path.shape[1]
    s = place[0]
    core = lax.rem(s, 2)
    run_copies(
        [
            pltpu.make_async_copy(path, p.at[pl.ds(2, images)], sems.at[0]),
            pltpu.make_async_copy(
                from_inner, p.at[pl.ds(jnp.where(core == 0, images + 2, 0), 2)], sems.at[1]
            ),
        ]
    )
    descend(p, r, images, s, segs, inside_ranges(n), inner_rows(images, core), ())
    p_row = jnp.where(core == 0, 2, images)
    r_row = jnp.where(core == 0, 2, images - 1)
    p2_row = jnp.where(core == 0, 2, 0)
    plan = list(zip(border_parts(p, r, n), (p_low, r_low, p_high, r_high))) + [
        (p.at[pl.ds(p_row, 2)], p_kept),
        (r.at[pl.ds(r_row, 2)], r_kept),
        (
            p.at[pl.ds(p2_row + 2, images - 2), pl.ds(4, n - 8)],
            p2.at[pl.ds(p2_row, images - 2)],
        ),
    ]
    run_copies([pltpu.make_async_copy(a, b, sems.at[i]) for i, (a, b) in enumerate(plan)])


def inside_b_kernel(
    segs,
    place,
    offsets,
    weights,
    from_outer,
    p_kept,
    r_kept,
    p2_in,
    p_low_in,
    r_low_in,
    p_high_in,
    r_high_in,
    p2,
    p_low,
    r_low,
    p_high,
    r_high,
    slots_all,
    slots_far,
    p,
    r,
    sems,
):
    del p_low_in, r_low_in, p_high_in, r_high_in
    images, n = p2_in.shape[0], p_kept.shape[1]
    s = place[0]
    core = lax.rem(s, 2)
    p2_row = jnp.where(core == 0, 2, 0)
    done = pltpu.make_async_copy(
        p2_in.at[pl.ds(p2_row, images - 2)],
        p.at[pl.ds(p2_row + 2, images - 2), pl.ds(4, n - 8)],
        sems.at[5],
    )
    done.start()
    run_copies(
        [
            pltpu.make_async_copy(
                from_outer, p.at[pl.ds(jnp.where(core == 0, 0, images + 2), 2)], sems.at[0]
            ),
            pltpu.make_async_copy(
                p_kept, p.at[pl.ds(jnp.where(core == 0, 2, images), 2)], sems.at[1]
            ),
            pltpu.make_async_copy(
                r_kept, r.at[pl.ds(jnp.where(core == 0, 2, images - 1), 2)], sems.at[2]
            ),
        ]
    )
    descend(p, r, images, s, segs, inside_ranges(n), outer_rows(images, core), ())
    done.wait()
    p_rows = pl.ds(jnp.where(core == 0, 0, images), 4)
    r_rows = pl.ds(jnp.where(core == 0, 0, images), 3)
    new_row = jnp.where(core == 0, 0, images - 2)
    parts = border_parts(p, r, n)
    plan = [
        (part.at[rows], out.at[rows])
        for part, out, rows in zip(
            parts, (p_low, r_low, p_high, r_high), (p_rows, r_rows, p_rows, r_rows)
        )
    ] + [(p.at[pl.ds(new_row + 2, 2), pl.ds(4, n - 8)], p2.at[pl.ds(new_row, 2)])]
    copies = [pltpu.make_async_copy(a, b, sems.at[i]) for i, (a, b) in enumerate(plan)]
    for c in copies:
        c.start()
    quarter = images // 4
    total = segs * images
    k0 = outer_base(s, images)
    for far in (False, True):

        def to_slots(i, x, far=far):
            row = i + (quarter if far else 0)
            k = jnp.minimum(k0 + row, total - 1)
            slot = mix(weights, offsets, k, p, 2, x + 4)
            slots_all[row, x] = slot
            if far:
                slots_far[i, x] = slot

        each_plane((0, quarter), (0, n - 8), to_slots)
    for c in copies:
        c.wait()


def edge_kernel(
    segs,
    tiles,
    low,
    place,
    offsets,
    weights,
    path,
    from_outer,
    from_inner,
    beyond,
    corner_outer,
    corner_inner,
    p_border,
    r_border,
    p2,
    slots,
    p,
    r,
    sems,
):
    images, n = path.shape[0], path.shape[1]
    s, t = place[0], place[1]
    core = lax.rem(s, 2)
    outer_near = jnp.where(core == 0, 1, images + 2)
    outer_far = jnp.where(core == 0, 0, images + 3)
    inner_near = jnp.where(core == 0, images + 2, 1)
    inner_far = jnp.where(core == 0, images + 3, 0)
    outer_row = jnp.where(core == 0, 0, images + 2)
    inner_row = jnp.where(core == 0, images + 2, 0)
    own, at = (pl.ds(0, 2), pl.ds(4, 2)) if low else (pl.ds(n - 2, 2), pl.ds(6, 2))
    three, two = (pl.ds(1, 3), pl.ds(2, 2)) if low else (pl.ds(8, 3), pl.ds(8, 2))
    plan = [
        (path.at[:, own], p.at[pl.ds(2, images), at]),
        (from_outer.at[:, own], p.at[pl.ds(outer_row, 2), at]),
        (from_inner.at[:, own], p.at[pl.ds(inner_row, 2), at]),
        (beyond, p.at[pl.ds(2, images), pl.ds(0 if low else 8, 4)]),
        (corner_outer.at[pl.ds(0, 3)], p.at[outer_near, three]),
        (corner_outer.at[pl.ds(3, 2)], p.at[outer_far, two]),
        (corner_inner.at[pl.ds(0, 3)], p.at[inner_near, three]),
        (corner_inner.at[pl.ds(3, 2)], p.at[inner_far, two]),
        (p_border, p.at[:, pl.ds(6 if low else 4, 2)]),
        (r_border, r.at[:, pl.ds(5 if low else 3, 4)]),
    ]
    run_copies([pltpu.make_async_copy(a, b, sems.at[i]) for i, (a, b) in enumerate(plan)])
    half = images // 2
    total = segs * images
    k0 = outer_base(s, images)
    outside = (t == 0, (1, 4)) if low else (t == tiles - 1, (8, 11))
    ranges = (((1, 5), (2, 6)), ((3, 7), (4, 8)))
    if not low:
        ranges = (((7, 11), (6, 10)), ((5, 9), (4, 8)))
    descend(p, r, images, s, segs, ranges, all_rows(images), (outside,))

    def to_slots(i, x):
        k = jnp.minimum(k0 + i, total - 1)
        slots[i, x] = mix(weights, offsets, k, p, 2, x + 4)

    each_plane((0, half), (0, 4), to_slots)

    def to_p2(j, x):
        p2[j, x] = p[j + 2, x + 4]

    each_plane((0, images), (0, 4), to_p2)


def corner_kernel(low, first_if_zero, place, src, out, sems):
    images, width = src.shape[0], src.shape[1]
    at_first = (lax.rem(place[0], 2) == 0) == first_if_zero
    near = jnp.where(at_first, 0, images - 1)
    far = jnp.where(at_first, 1, images - 2)
    three, two = (pl.ds(0, 3), pl.ds(0, 2)) if low else (pl.ds(width - 3, 3), pl.ds(width - 2, 2))
    run_copies(
        [
            pltpu.make_async_copy(src.at[near, three], out.at[pl.ds(0, 3)], sems.at[0]),
            pltpu.make_async_copy(src.at[far, two], out.at[pl.ds(3, 2)], sems.at[1]),
        ]
    )


def pair_kernel(first_if_zero, place, path, out, sems):
    images = path.shape[0]
    at_first = (lax.rem(place[0], 2) == 0) == first_if_zero
    first = jnp.where(at_first, 0, images - 2)
    run_copies([pltpu.make_async_copy(path.at[pl.ds(first, 2)], out, sems.at[0])])


def plane_parts(n):
    return ((0, 4, 0), (4, n - 4, 1), (n - 4, n, 2))


def inner_slots_kernel(place, offsets, weights, low, inside, high, slots):
    images, n = inside.shape[0], slots.shape[1]
    half = images // 2
    k0 = inner_base(place[0], images)
    for lo, hi, which in plane_parts(n):
        p = (low, inside, high)[which]

        def body(i, x):
            slots[i, x + lo] = mix(weights, offsets, k0 + i, p, 0, x)

        each_plane((0, half), (0, hi - lo), body)


def own_kernel(place, offsets, weights, low, inside, high, out):
    images, n = out.shape[0], out.shape[1]
    k0 = place[0] * images
    for lo, hi, which in plane_parts(n):
        p = (low, inside, high)[which]

        def body(i, x):
            out[i, x + lo] = mix(weights, offsets, k0 + i, p, 0, x)

        each_plane((0, images), (0, hi - lo), body)


def bounds(segs, counts, s):
    before = jnp.int32(0)
    end = jnp.int32(0)
    for i in range(segs):
        before = before + jnp.where(i < s, counts[i], 0)
        end = end + jnp.where(i <= s, counts[i], 0)
    return before, end


def choose_kernel(segs, place, counts, slots, lent, out, sems):
    s = place[0]
    images = 2 * slots.shape[0]
    near = slots.at[pl.ds(0, lent.shape[0])]
    before, end = bounds(segs, counts, s)
    gives = jnp.where(lax.rem(s, 2) == 0, before < s * images, end > (s + 1) * images)

    @pl.when(gives)
    def _():
        run_copies([pltpu.make_async_copy(near, out, sems.at[0])])

    @pl.when(jnp.logical_not(gives))
    def _():
        run_copies([pltpu.make_async_copy(lent, out, sems.at[0])])


def place_kernel(
    segs, early, place, counts, low, inside, near, back, high, inner_part, own, out, sems
):
    del own
    images, n = out.shape[0], out.shape[1]
    half = images // 2
    quarter = half // 2
    s = place[0]
    core = lax.rem(s, 2)
    before, end = bounds(segs, counts, s)
    is_z = lax.rem(lax.div(s + 1, 2), 2) == 1

    def copies(i, slot, from_outer, straight):
        for lo, hi, which in plane_parts(n):
            returned = which == 1 and not straight and slot >= quarter
            if from_outer and (which == 2 or returned) == early:
                continue
            if from_outer and which == 1 and not straight:
                src = (near if slot < quarter else back).at[slot % quarter]
            elif from_outer:
                src = (low, inside, high)[which].at[slot]
            else:
                src = inner_part.at[slot, pl.ds(lo, hi - lo)]
            yield pltpu.make_async_copy(src, out.at[i, pl.ds(lo, hi - lo)], sems.at[i, which])

    for start in (True, False):
        for i in range(images):
            k = s * images + i
            slot = i % half
            foreign = (k < before) if i < half else (k >= end)
            outer_core = 0 if i < half else 1

            cases = [((core == outer_core) & is_z, True, True)]
            cases += [((core == outer_core) & jnp.logical_not(is_z), True, False)]
            if early:
                cases += [(core != outer_core, False, None)]
            for cond, from_outer, straight in cases:

                @pl.when(foreign & cond)
                def _(i=i, slot=slot, from_outer=from_outer, straight=straight):
                    for c in copies(i, slot, from_outer, straight):
                        if start:
                            c.start()
                        else:
                            c.wait()


def field(*shape):
    return jax.ShapeDtypeStruct(shape, jnp.float32)


def cost(planes, arrays):
    return pl.CostEstimate(
        flops=planes * 8192 * 60, bytes_accessed=arrays * 2**20, transcendentals=0
    )


def params(mib):
    return pltpu.CompilerParams(vmem_limit_bytes=mib * 2**20)


def step(path_field, counts, offsets, weights):
    images, n, gy, gz = path_field.shape
    segs, tiles = lax.axis_size("seg"), lax.axis_size("tile")
    s, t = lax.axis_index("seg"), lax.axis_index("tile")
    half = images // 2
    place = jnp.stack([s, t]).astype(jnp.int32)

    def send(block, ds_of, dt):
        dt_of = dt if callable(dt) else lambda _: dt
        return lax.ppermute(block, AXES, routes(segs, tiles, ds_of, dt_of))

    def across(tile):
        return -1 if tile % 2 else 1

    def stay(_):
        return 0

    def call(kernel, *args, **settings):
        return pl.pallas_call(kernel, **settings)(*args)

    def corner(array, low, first_if_zero):
        return call(
            functools.partial(corner_kernel, low, first_if_zero),
            place,
            array,
            out_shape=field(5, gy, gz),
            in_specs=[SMEM, ANY],
            out_specs=VMEM,
            scratch_shapes=[pltpu.SemaphoreType.DMA((2,))],
            compiler_params=params(1),
            cost_estimate=cost(0, 1),
        )

    def pair(first_if_zero):
        return call(
            functools.partial(pair_kernel, first_if_zero),
            place,
            path_field,
            out_shape=field(2, n, gy, gz),
            in_specs=[SMEM, ANY],
            out_specs=VMEM,
            scratch_shapes=[pltpu.SemaphoreType.DMA((1,))],
            compiler_params=params(2),
            cost_estimate=cost(0, 2),
        )

    from_outer = send(pair(True), outer, 0)
    from_inner = send(pair(False), inner, 0)
    below = send(path_field[:, n - 4 :], stay, 1)
    above = send(path_field[:, :4], stay, -1)
    corner_below = send(corner(path_field, False, True), outer, 1)
    corner_above = send(corner(path_field, True, True), outer, -1)

    border = (field(images + 4, 2, gy, gz), field(images + 3, 4, gy, gz))
    levels = [
        pltpu.VMEM((images + 4, n, gy, gz), jnp.float32),
        pltpu.VMEM((images + 3, n, gy, gz), jnp.float32),
        pltpu.SemaphoreType.DMA((7,)),
    ]
    *first, p_kept, r_kept = call(
        functools.partial(inside_a_kernel, segs),
        place,
        path_field,
        from_inner,
        out_shape=(field(images, n - 8, gy, gz),)
        + border * 2
        + (field(2, n, gy, gz), field(2, n, gy, gz)),
        in_specs=[SMEM, ANY, ANY],
        out_specs=(ANY,) * 7,
        scratch_shapes=levels,
        compiler_params=params(14),
        cost_estimate=cost(36 * 10, 8),
    )
    p2_inside, *borders, slots_all, slots_far = call(
        functools.partial(inside_b_kernel, segs),
        place,
        offsets,
        weights,
        from_outer,
        p_kept,
        r_kept,
        *first,
        out_shape=(field(images, n - 8, gy, gz),) + border * 2
        + (field(half, n - 8, gy, gz), field(half // 2, n - 8, gy, gz)),
        in_specs=[SMEM, SMEM, SMEM] + [ANY] * 8,
        out_specs=(ANY,) * 5 + (VMEM,) * 2,
        input_output_aliases={6 + i: i for i in range(5)},
        scratch_shapes=levels,
        compiler_params=params(14),
        cost_estimate=cost(9 * 10, 6),
    )
    lent = send(slots_far, along_y, across)
    chosen = call(
        functools.partial(choose_kernel, segs),
        place,
        counts,
        slots_all,
        lent,
        out_shape=field(half // 2, n - 8, gy, gz),
        in_specs=[SMEM, SMEM, ANY, ANY],
        out_specs=VMEM,
        scratch_shapes=[pltpu.SemaphoreType.DMA((1,))],
        compiler_params=params(1),
        cost_estimate=cost(0, 1),
    )
    got_near = send(chosen, along_y, 0)
    got_inside = send(slots_all, along_z, 0)
    got_back = send(got_near, along_y, across)

    def edge(low, beyond, corner_outer):
        corner_inner = send(corner(beyond, not low, False), inner, 0)
        return call(
            functools.partial(edge_kernel, segs, tiles, low),
            place,
            offsets,
            weights,
            path_field,
            from_outer,
            from_inner,
            beyond,
            corner_outer,
            corner_inner,
            *(borders[:2] if low else borders[2:]),
            out_shape=(field(images, 4, gy, gz), field(half, 4, gy, gz)),
            in_specs=[SMEM, SMEM, SMEM] + [ANY] * 8,
            out_specs=(VMEM, VMEM),
            scratch_shapes=[
                pltpu.VMEM((images + 4, 12, gy, gz), jnp.float32),
                pltpu.VMEM((images + 3, 12, gy, gz), jnp.float32),
                pltpu.SemaphoreType.DMA((10,)),
            ],
            compiler_params=params(14),
            cost_estimate=cost(28 * 10, 6),
        )

    p2_low, slots_low = edge(True, below, corner_below)
    got_low = send(slots_low, outer, 0)
    p2_high, slots_high = edge(False, above, corner_above)
    got_high = send(slots_high, outer, 0)

    slots_inner = call(
        inner_slots_kernel,
        place,
        offsets,
        weights,
        p2_low,
        p2_inside,
        p2_high,
        out_shape=field(half, n, gy, gz),
        in_specs=[SMEM, SMEM, SMEM, VMEM, VMEM, VMEM],
        out_specs=VMEM,
        compiler_params=params(8),
        cost_estimate=cost(16, 6),
    )
    got_inner = send(slots_inner, inner, 0)
    own = call(
        own_kernel,
        place,
        offsets,
        weights,
        p2_low,
        p2_inside,
        p2_high,
        out_shape=field(images, n, gy, gz),
        in_specs=[SMEM, SMEM, SMEM, VMEM, VMEM, VMEM],
        out_specs=VMEM,
        compiler_params=params(10),
        cost_estimate=cost(32, 8),
    )

    def put(early, base):
        last = got_high if not early else p2_high
        back = got_back if not early else got_near
        return call(
            functools.partial(place_kernel, segs, early),
            place,
            counts,
            got_low,
            got_inside,
            got_near,
            back,
            last,
            got_inner,
            base,
            out_shape=field(images, n, gy, gz),
            in_specs=[SMEM, SMEM] + [ANY] * 7,
            out_specs=ANY,
            scratch_shapes=[pltpu.SemaphoreType.DMA((images, 3))],
            input_output_aliases={8: 0},
            compiler_params=params(1),
            cost_estimate=cost(2, 4),
        )

    return put(False, put(True, own))


def solution(mesh):
    return jax.shard_map(
        step,
        mesh=mesh,
        in_specs=(P("seg", "tile", None, None), P(), P(), P()),
        out_specs=P("seg", "tile", None, None),
        check_vma=False,
    )
```
